128 devices in a mesh: dp: 16 (over y, x), chan: 8 (over z, core).
Axes of the slice: x: 4, y: 4, z: 4, core: 2. Of those that a mesh axis runs over, the one named last changes fastest.
Arguments:
- signal: bfloat16 [16, 512, 8192], P('dp', 'chan'), may hold values from -6 to 6
- signal_grad: bfloat16 [16, 512, 8192], P('dp', 'chan'), may hold values from -6 to 6
- embed_weight: float32 [64, 33], replicated, may hold values from -1 to 1
- embed_bias: float32 [64], replicated, may hold values from -3.140625 to 3.140625
- hidden_weight: float32 [64, 64], replicated, may hold values from -0.75 to 0.75
- frequency: float32 [2, 64], replicated, may hold values from 0.5 to 2
- output_weight: float32 [512, 64], replicated, may hold values from -0.75 to 0.75
- decay_rate: float32 [512], replicated, may hold values from 0.3 to 30
Outputs:
- filter_grad: float32 [512, 16384], P(None, ('dp', 'chan'))
- embed_grad: float32 [64, 33], replicated
- bias_grad: float32 [64], replicated
- hidden_grad: float32 [64, 64], replicated
- frequency_grad: float32 [2, 64], replicated
- output_grad: float32 [512, 64], replicated
- decay_grad: float32 [512], replicated
The draws below stay inside these ranges and needn't reach their ends.
All inputs are finite; a program needn't handle non-finite values.
Results may differ from the reference program's by a relative error of at most 0.0003.
Values may be sent and summed in bfloat16 or wider, within the bound.
A program may use at most 64 MiB of HBM per device.

```python
import math
import jax
import jax.numpy as jnp
from jax import lax

CH = 512
HID = 64
L = 8192
EMB = 33
SEQS = 16


def shard_levels(own_key, shape, shards, least, top_value):
    level, own = 1.0, jax.random.fold_in(own_key, 6)
    for axis_at, blocks in shards:
        steps = jnp.exp(jax.random.uniform(jax.random.fold_in(own, axis_at), (blocks,), jnp.float32, least / len(shards), top_value / len(shards)))
        level = level * jnp.repeat(steps, shape[axis_at] // blocks).reshape([-1 if axis == axis_at else 1 for axis in range(len(shape))])
    return level


def noise(stream_key, shape, width, most, split=(), kind=jnp.bfloat16):
    values = width * jax.random.normal(stream_key, shape, jnp.float32)
    if split:
        values = values * shard_levels(stream_key, shape, split, -0.22, 0.18)
    return jnp.clip(values, -most, most).astype(kind)


def setup_inputs(seed: int = 0) -> dict:
    keys = jax.random.split(jax.random.key(seed), 9)
    signal = noise(keys[0], (SEQS, CH, L), 1.0, 6.0, ((0, 16), (1, 8)))
    signal_grad = noise(keys[1], (SEQS, CH, L), 1.0, 6.0, ((0, 16), (1, 8)))
    embed_weight = noise(keys[2], (HID, EMB), EMB ** -0.5, 1.0, (), jnp.float32)
    embed_bias = jnp.clip(jax.random.uniform(keys[3], (HID,), jnp.float32, -3.140625, 3.140625), -3.140625, 3.140625)
    hidden_weight = noise(keys[4], (HID, HID), HID ** -0.5, 0.75, (), jnp.float32)
    frequency = jnp.clip(jnp.exp(jax.random.uniform(keys[5], (2, HID), jnp.float32, math.log(0.5), math.log(2.0))), 0.5, 2.0)
    output_weight = noise(keys[6], (CH, HID), HID ** -0.5, 0.75, (), jnp.float32)
    decay_rate = jnp.clip(jnp.exp(jax.random.uniform(keys[7], (CH,), jnp.float32, math.log(0.3), math.log(30.0))), 0.3, 30.0)
    return dict(signal=signal, signal_grad=signal_grad, embed_weight=embed_weight, embed_bias=embed_bias, hidden_weight=hidden_weight, frequency=frequency, output_weight=output_weight, decay_rate=decay_rate)


def lag_features(lag, length, bands):
    total = 2 * length
    scaled = lag.astype(jnp.float32) / length
    sines = []
    cosines = []
    for band in range(bands):
        factor = max(1, int(0.45 * total * 10000.0 ** (-band / bands)))
        phase = (lag * factor % total).astype(jnp.float32) * (2.0 * math.pi / total)
        sines.append(jnp.sin(phase))
        cosines.append(jnp.cos(phase))
    return jnp.stack([scaled] + sines + cosines)

def filter_loss(params, lag, cotangent, length):
    embed_weight, embed_bias, hidden_weight, frequency, output_weight, decay_rate = params
    bands = (embed_weight.shape[1] - 1) // 2
    exact = lax.Precision.HIGHEST
    table = lag_features(lag, length, bands)
    first = jnp.sin(frequency[0][:, None] * (jnp.dot(embed_weight, table, precision=exact, preferred_element_type=jnp.float32) + embed_bias[:, None]))
    second = jnp.sin(frequency[1][:, None] * jnp.dot(hidden_weight, first, precision=exact, preferred_element_type=jnp.float32))
    shaped = jnp.dot(output_weight, second, precision=exact, preferred_element_type=jnp.float32)
    window = jnp.exp(-decay_rate[:, None] * jnp.abs(lag).astype(jnp.float32)[None, :] / length)
    return jnp.sum(shaped * window * cotangent) / math.sqrt(2 * length)

def reference(signal, signal_grad, embed_weight, embed_bias, hidden_weight, frequency, output_weight, decay_rate):
    total = 2 * L
    block = 32 if CH % 32 == 0 else CH

    def one_block(index):
        start = index * block
        inputs = lax.dynamic_slice_in_dim(signal, start, block, 1).astype(jnp.float32)
        grads = lax.dynamic_slice_in_dim(signal_grad, start, block, 1).astype(jnp.float32)
        spectrum_in = jnp.fft.rfft(inputs, n=total, axis=-1)
        spectrum_grad = jnp.fft.rfft(grads, n=total, axis=-1)
        cross = lax.optimization_barrier(jnp.sum(jnp.conj(spectrum_in) * spectrum_grad, axis=0))
        return jnp.fft.irfft(cross, n=total, axis=-1)
    blocks = lax.map(one_block, jnp.arange(CH // block, dtype=jnp.int32))
    filter_grad = blocks.reshape(CH, total) / math.sqrt(SEQS * L)
    position = jnp.arange(total, dtype=jnp.int32)
    lag = jnp.where(position < L, position, position - total)
    params = (embed_weight, embed_bias, hidden_weight, frequency, output_weight, decay_rate)
    grads = jax.grad(filter_loss)(params, lag, filter_grad, L)
    return (filter_grad, grads[0], grads[1], grads[2], grads[3], grads[4], grads[5])
```

```python
import math

import jax
import jax.numpy as jnp
import numpy as np
from jax import lax
from jax.experimental import pallas as pl
from jax.experimental.pallas import tpu as pltpu
from jax.sharding import Mesh
from jax.sharding import PartitionSpec as P

DP = ("y", "x")
CHAN = ("z", "core")
MESH_ID = pl.DeviceIdType.MESH
OFFSETS = sorted(
    [(dy, dx) for dy in range(4) for dx in range(4)],
    key=lambda p: (min(p[0], 4 - p[0]) + min(p[1], 4 - p[1])),
)
PEERS = [(dz, dc) for dz in range(4) for dc in range(2)]


def split_table(values):
    high = values.astype(jnp.bfloat16)
    low = (values - high.astype(np.float64)).astype(jnp.bfloat16)
    return high, low


def transform_tables(total, scale):
    half, side = 64, 128
    k1 = np.arange(half)[:, None] + 0.5
    n1 = np.arange(half)[None, :]
    angle = -2.0 * np.pi * k1 * n1 / side
    first = np.concatenate([np.cos(angle), np.sin(angle)], axis=0)
    first = np.concatenate(split_table(first), axis=1)
    n2 = np.arange(side)[None, :]
    angle = -2.0 * np.pi * k1 * n2 / total
    twist = np.stack([np.cos(angle), np.sin(angle)]).astype(np.float32)
    rows = np.arange(side)[:, None]
    angle = -2.0 * np.pi * (rows * n2 % side) / side
    cosine, sine = np.cos(angle), np.sin(angle)
    forward = np.block([[cosine, sine], [-sine, cosine]])
    high, low = split_table(forward)
    forward = np.concatenate([high, high, low], axis=0)
    backward = np.block([[cosine, -sine], [sine, cosine]])
    high, low = split_table(backward)
    backward = np.concatenate([high, high, low], axis=0)
    lag_row = np.arange(side)[:, None]
    freq = np.arange(half)[None, :] + 0.5
    angle = 2.0 * np.pi * lag_row * freq / side
    last = np.concatenate([np.cos(angle), -np.sin(angle)], axis=1)
    last = last * np.where(lag_row < half, 1.0, -1.0) * (2.0 * scale / total)
    high, low = split_table(last)
    last = np.concatenate([high, high, low], axis=1)
    return first, twist, forward, backward, last


def split_values(values):
    high = values.astype(jnp.bfloat16)
    low = (values - high.astype(jnp.float32)).astype(jnp.bfloat16)
    return high, low


def dot(a, b):
    return jnp.dot(a, b, preferred_element_type=jnp.float32)


def correlate_kernel(
    both,
    first,
    twist,
    forward,
    backward,
    last,
    out,
    arrived,
    spectrum,
    lags,
    mine,
    rows,
    landed,
    local_sem,
    send_sem,
    recv_sem,
    send2_sem,
    recv2_sem,
    send3_sem,
    recv3_sem,
):
    y, x = lax.axis_index("y"), lax.axis_index("x")
    z, core = lax.axis_index("z"), lax.axis_index("core")
    me = y * 4 + x
    group = z * 2 + core

    barrier = pltpu.get_barrier_semaphore()
    dp_peers = []
    for dy, dx in OFFSETS[1:]:
        ty, tx = lax.rem(y + dy, 4), lax.rem(x + dx, 4)
        dp_peers.append((ty * 4 + tx, {"y": ty, "x": tx}))
    chan_peers = []
    for dz, dc in PEERS[1:]:
        tz, tc = lax.rem(z + dz, 4), lax.rem(core + dc, 2)
        chan_peers.append((tz * 2 + tc, {"z": tz, "core": tc}))
    for _, where in dp_peers + chan_peers:
        pl.semaphore_signal(barrier, 1, device_id=where, device_id_type=MESH_ID)
    own = pltpu.make_async_copy(both.at[me], arrived.at[0], local_sem)
    own.start()
    spectrum[...] = jnp.zeros_like(spectrum)
    pl.semaphore_wait(barrier, len(dp_peers) + len(chan_peers))

    copies = []
    for at, (index, where) in enumerate(dp_peers):
        copy = pltpu.make_async_remote_copy(
            both.at[index],
            arrived.at[at + 1],
            send_sem.at[at],
            recv_sem.at[at],
            device_id=where,
            device_id_type=MESH_ID,
        )
        copy.start()
        copies.append(copy)

    cos_t, sin_t = twist[0], twist[1]

    def add_sequence(slot):
        parts = []
        for part in range(2):
            for channel in range(4):
                data = arrived[slot, channel, part]
                data = jnp.concatenate([data, data], axis=0)
                step = dot(first[...], data)
                real, imag = step[:64], step[64:]
                parts.append(
                    jnp.concatenate(
                        [real * cos_t - imag * sin_t, real * sin_t + imag * cos_t], axis=1
                    )
                )
        high, low = split_values(jnp.concatenate(parts, axis=0))
        whole = dot(jnp.concatenate([high, low, high], axis=1), forward[...])
        in_real, in_imag = whole[:256, :128], whole[:256, 128:]
        grad_real, grad_imag = whole[256:, :128], whole[256:, 128:]
        spectrum[:, :128] += in_real * grad_real + in_imag * grad_imag
        spectrum[:, 128:] += in_real * grad_imag - in_imag * grad_real

    own.wait()
    add_sequence(0)

    @pl.loop(0, 15)
    def _(at):
        pltpu.make_async_remote_copy(
            both.at[0],
            arrived.at[at + 1],
            send_sem.at[at],
            recv_sem.at[at],
            device_id={"y": y, "x": lax.rem(x + 1, 4)},
            device_id_type=MESH_ID,
        ).wait_recv()
        add_sequence(at + 1)

    high, low = split_values(spectrum[...])
    back = dot(jnp.concatenate([high, low, high], axis=1), backward[...])
    columns = []
    for channel in range(4):
        real = back[64 * channel : 64 * channel + 64, :128]
        imag = back[64 * channel : 64 * channel + 64, 128:]
        columns.append(
            jnp.concatenate([real * cos_t + imag * sin_t, imag * cos_t - real * sin_t], axis=0)
        )
    high, low = split_values(jnp.concatenate(columns, axis=1))
    result = dot(last[...], jnp.concatenate([high, low, high], axis=0))
    lags[...] = result.reshape(16, 8, 512)

    for copy in copies:
        copy.wait_send()

    copies = []
    for at, (index, where) in enumerate(dp_peers):
        copy = pltpu.make_async_remote_copy(
            lags.at[index],
            mine.at[me],
            send2_sem.at[at],
            recv2_sem.at[at],
            device_id=where,
            device_id_type=MESH_ID,
        )
        copy.start()
        copies.append(copy)
    mine[me] = lags[me]
    for copy in copies:
        copy.wait()

    for lag_row in range(8):
        for channel in range(4):
            rows[lag_row, pl.ds(channel, 16, stride=4), :] = mine[
                :, lag_row, 128 * channel : 128 * channel + 128
            ]

    copies = []
    for at, (index, where) in enumerate(chan_peers):
        copy = pltpu.make_async_remote_copy(
            rows.at[index],
            landed.at[group],
            send3_sem.at[at],
            recv3_sem.at[at],
            device_id=where,
            device_id_type=MESH_ID,
        )
        copy.start()
        copies.append(copy)
    landed[group] = rows[group]
    for copy in copies:
        copy.wait()
    out[...] = landed[...].reshape(512, 128)


def correlate(signal, signal_grad, total, scale):
    both = jnp.stack(
        [signal.reshape(16, 4, 64, 128), signal_grad.reshape(16, 4, 64, 128)], axis=2
    )
    tables = transform_tables(total, scale)
    vmem = pl.BlockSpec(memory_space=pltpu.VMEM)
    return pl.pallas_call(
        correlate_kernel,
        out_shape=jax.ShapeDtypeStruct((512, 128), jnp.float32),
        in_specs=[pl.BlockSpec(memory_space=pl.ANY)] + [vmem] * 5,
        out_specs=vmem,
        scratch_shapes=[
            pltpu.VMEM((16, 4, 2, 64, 128), jnp.bfloat16),
            pltpu.VMEM((256, 256), jnp.float32),
            pltpu.VMEM((16, 8, 512), jnp.float32),
            pltpu.VMEM((16, 8, 512), jnp.float32),
            pltpu.VMEM((8, 64, 128), jnp.float32),
            pltpu.VMEM((8, 64, 128), jnp.float32),
            pltpu.SemaphoreType.DMA,
            pltpu.SemaphoreType.DMA((15,)),
            pltpu.SemaphoreType.DMA((15,)),
            pltpu.SemaphoreType.DMA((15,)),
            pltpu.SemaphoreType.DMA((15,)),
            pltpu.SemaphoreType.DMA((7,)),
            pltpu.SemaphoreType.DMA((7,)),
        ],
        compiler_params=pltpu.CompilerParams(
            collective_id=0, has_side_effects=True, vmem_limit_bytes=32 * 1024 * 1024
        ),
    )(both, *[jnp.asarray(t) for t in tables])


def split_up(x, dim, peers):
    shape = x.shape
    blocks = x.reshape(*shape[:dim], peers, shape[dim] // peers, *shape[dim + 1 :])
    return jnp.moveaxis(blocks, dim, 0)


def laid_out(blocks, dim):
    shape = list(blocks.shape[1:])
    shape[dim] *= blocks.shape[0]
    return jnp.moveaxis(blocks, 0, dim).reshape(shape)


def sum_at_owner(x, axis, dim):
    blocks = split_up(x, dim, lax.axis_size(axis))
    arrived = lax.all_to_all(blocks, axis, split_axis=0, concat_axis=0, tiled=True)
    return arrived.sum(axis=0)


def summed_rows(x, axes, dim):
    far, near = axes
    blocks = split_up(x, dim, lax.axis_size(far))
    nearer = sum_at_owner(blocks, near, dim + 1)
    arrived = lax.all_to_all(nearer, far, split_axis=0, concat_axis=0, tiled=True)
    return arrived.sum(axis=0)


def filled_up(lines, peers):
    spare = -len(lines) % peers
    return jnp.pad(lines, [(0, spare)] + [(0, 0)] * (lines.ndim - 1))


def copy_for_each(x, axis):
    peers = lax.axis_size(axis)
    return lax.all_to_all(jnp.broadcast_to(x[None], (peers, *x.shape)), axis, 0, 0, tiled=True)


def gathered_by_axis(x, axes, dim):
    far, near = axes
    blocks = copy_for_each(copy_for_each(x, far), near)
    return laid_out(blocks.swapaxes(0, 1).reshape(-1, *x.shape), dim)


def total_of(x, axes):
    own = summed_rows(filled_up(x, lax.axis_size(axes[0]) * lax.axis_size(axes[1])), axes, 0)
    whole = gathered_by_axis(own, axes, 0)
    return whole[: len(x)].reshape(x.shape)


def together(arrays, axis):
    vector, at, finished = (jnp.concatenate([a.reshape(-1) for a in arrays]), 0, [])
    running = total_of(vector, axis)
    for a in arrays:
        finished.append(running[at : at + a.size].reshape(a.shape))
        at += a.size
    return tuple(finished)


def lag_features(lag, length, bands):
    total = 2 * length
    scaled = lag.astype(jnp.float32) / length
    sines = []
    cosines = []
    for band in range(bands):
        factor = max(1, int(0.45 * total * 10000.0 ** (-band / bands)))
        phase = (lag * factor % total).astype(jnp.float32) * (2.0 * math.pi / total)
        sines.append(jnp.sin(phase))
        cosines.append(jnp.cos(phase))
    return jnp.stack([scaled] + sines + cosines)


def filter_loss(params, lag, cotangent, length):
    embed_weight, embed_bias, hidden_weight, frequency, output_weight, decay_rate = params
    bands = (embed_weight.shape[1] - 1) // 2
    exact = lax.Precision.HIGHEST
    table = lag_features(lag, length, bands)
    first = jnp.sin(
        frequency[0][:, None]
        * (
            jnp.dot(embed_weight, table, precision=exact, preferred_element_type=jnp.float32)
            + embed_bias[:, None]
        )
    )
    second = jnp.sin(
        frequency[1][:, None]
        * jnp.dot(hidden_weight, first, precision=exact, preferred_element_type=jnp.float32)
    )
    shaped = jnp.dot(output_weight, second, precision=exact, preferred_element_type=jnp.float32)
    window = jnp.exp(-decay_rate[:, None] * jnp.abs(lag).astype(jnp.float32)[None, :] / length)
    return jnp.sum(shaped * window * cotangent) / math.sqrt(2 * length)


def local(
    signal,
    signal_grad,
    embed_weight,
    embed_bias,
    hidden_weight,
    frequency,
    output_weight,
    decay_rate,
):
    _, _, length = signal.shape
    total = 2 * length
    scale = 1.0 / math.sqrt(16 * length)
    filter_grad = correlate(signal[0], signal_grad[0], total, scale)
    lag_count = filter_grad.shape[1]
    device_rank = lax.axis_index(DP) * lax.axis_size(CHAN) + lax.axis_index(CHAN)
    position = device_rank * lag_count + jnp.arange(lag_count, dtype=jnp.int32)
    lag = jnp.where(position < length, position, position - total)
    params = (embed_weight, embed_bias, hidden_weight, frequency, output_weight, decay_rate)
    grads = jax.grad(filter_loss)(params, lag, filter_grad, length)
    summed = together(grads, (("y", "x", "z"), "core"))
    return (filter_grad, *summed)


def solution(mesh):
    torus = Mesh(mesh.devices.reshape(4, 4, 4, 2), ("y", "x", "z", "core"))
    return jax.shard_map(
        local,
        mesh=torus,
        in_specs=(P(DP, CHAN, None), P(DP, CHAN, None), P(), P(), P(), P(), P(), P()),
        out_specs=(P(None, DP + CHAN), P(), P(), P(), P(), P(), P()),
        check_vma=False,
    )
```

```python
import math

import jax
import jax.numpy as jnp
import numpy as np
from jax import lax
from jax.experimental import pallas as pl
from jax.experimental.pallas import tpu as pltpu
from jax.sharding import Mesh
from jax.sharding import PartitionSpec as P

DP = ("y", "x")
CHAN = ("z", "core")
MESH_ID = pl.DeviceIdType.MESH
OFFSETS = sorted(
    [(dy, dx) for dy in range(4) for dx in range(4)],
    key=lambda p: (min(p[0], 4 - p[0]) + min(p[1], 4 - p[1])),
)
PEERS = [(dz, dc) for dz in range(4) for dc in range(2)]


def split_table(values):
    high = values.astype(jnp.bfloat16)
    low = (values - high.astype(np.float64)).astype(jnp.bfloat16)
    return high, low


def transform_tables(total, scale):
    half, side = 64, 128
    k1 = np.arange(half)[:, None] + 0.5
    n1 = np.arange(half)[None, :]
    angle = -2.0 * np.pi * k1 * n1 / side
    first = np.concatenate([np.cos(angle), np.sin(angle)], axis=0)
    first = np.concatenate(split_table(first), axis=1)
    n2 = np.arange(side)[None, :]
    angle = -2.0 * np.pi * k1 * n2 / total
    twist = np.stack([np.cos(angle), np.sin(angle)]).astype(np.float32)
    rows = np.arange(side)[:, None]
    angle = -2.0 * np.pi * (rows * n2 % side) / side
    cosine, sine = np.cos(angle), np.sin(angle)
    forward = np.block([[cosine, sine], [-sine, cosine]])
    high, low = split_table(forward)
    forward = np.concatenate([high, high, low], axis=0)
    backward = np.block([[cosine, -sine], [sine, cosine]])
    high, low = split_table(backward)
    backward = np.concatenate([high, high, low], axis=0)
    lag_row = np.arange(side)[:, None]
    freq = np.arange(half)[None, :] + 0.5
    angle = 2.0 * np.pi * lag_row * freq / side
    last = np.concatenate([np.cos(angle), -np.sin(angle)], axis=1)
    last = last * np.where(lag_row < half, 1.0, -1.0) * (2.0 * scale / total)
    high, low = split_table(last)
    last = np.concatenate([high, high, low], axis=1)
    return first, twist, forward, backward, last


def split_values(values):
    high = values.astype(jnp.bfloat16)
    low = (values - high.astype(jnp.float32)).astype(jnp.bfloat16)
    return high, low


def dot(a, b):
    return jnp.dot(a, b, preferred_element_type=jnp.float32)


def exact_dot(a, b, dims=((1,), (0,))):
    return lax.dot_general(
        a, b, (dims, ((), ())), precision=lax.Precision.HIGHEST, preferred_element_type=jnp.float32
    )


def sine_cosine(angle):
    turns = jnp.floor(angle * (2.0 / math.pi) + 0.5)
    rest = angle - turns * 1.5703125
    rest = rest - turns * 4.837512969970703125e-4
    rest = rest - turns * 7.54978995489188216e-8
    square = rest * rest
    sine = -1.9515295891e-4 * square + 8.3321608736e-3
    sine = sine * square - 1.6666654611e-1
    sine = sine * square * rest + rest
    cosine = 2.443315711809948e-5 * square - 1.388731625493765e-3
    cosine = cosine * square + 4.166664568298827e-2
    cosine = cosine * square * square - 0.5 * square + 1.0
    quarter = turns.astype(jnp.int32)
    odd = (quarter & 1) == 1
    first = jnp.where(odd, cosine, sine)
    second = jnp.where(odd, sine, cosine)
    first = jnp.where((quarter & 2) == 2, -first, first)
    second = jnp.where(((quarter + 1) & 2) == 2, -second, second)
    return first, second


def as_columns(row):
    return jnp.broadcast_to(row, (128, row.shape[1])).T


def kernel(
    both,
    first,
    twist,
    forward,
    backward,
    last,
    bands,
    embed_weight,
    embed_bias,
    hidden_weight,
    frequency,
    output_weight,
    decay_rate,
    filter_out,
    embed_out,
    bias_out,
    hidden_out,
    frequency_out,
    output_out,
    decay_out,
    arrived,
    spectrum,
    lags,
    mine,
    rows,
    landed,
    table,
    embed_pad,
    decay_columns,
    pre_first,
    sine_first,
    cosine_first,
    pre_second,
    sine_second,
    cosine_second,
    window,
    slope,
    partial,
    partials,
    own_sum,
    group_sums,
    piece,
    pieces,
    local_sem,
    dp_send,
    dp_recv,
    chan_send,
    chan_recv,
):
    y, x = lax.axis_index("y"), lax.axis_index("x")
    z, core = lax.axis_index("z"), lax.axis_index("core")
    me = y * 4 + x
    group = z * 2 + core

    barrier = pltpu.get_barrier_semaphore()
    dp_peers = []
    for dy, dx in OFFSETS[1:]:
        ty, tx = lax.rem(y + dy, 4), lax.rem(x + dx, 4)
        dp_peers.append((ty * 4 + tx, {"y": ty, "x": tx}))
    chan_peers = []
    for dz, dc in PEERS[1:]:
        tz, tc = lax.rem(z + dz, 4), lax.rem(core + dc, 2)
        chan_peers.append((tz * 2 + tc, {"z": tz, "core": tc}))
    for _, where in dp_peers + chan_peers:
        pl.semaphore_signal(barrier, 1, device_id=where, device_id_type=MESH_ID)
    own = pltpu.make_async_copy(both.at[me], arrived.at[0], local_sem)
    own.start()
    spectrum[...] = jnp.zeros_like(spectrum)
    pl.semaphore_wait(barrier, len(dp_peers) + len(chan_peers))

    def exchange(stage, peers, sends, recvs, source, target):
        copies = []
        for at, (index, where) in enumerate(peers):
            copy = pltpu.make_async_remote_copy(
                source(index),
                target(at),
                sends.at[stage, at],
                recvs.at[stage, at],
                device_id=where,
                device_id_type=MESH_ID,
            )
            copy.start()
            copies.append(copy)
        return copies

    over_dp = lambda stage, source, target: exchange(
        stage, dp_peers, dp_send, dp_recv, source, target
    )
    over_chan = lambda stage, source, target: exchange(
        stage, chan_peers, chan_send, chan_recv, source, target
    )

    inputs = over_dp(0, lambda index: both.at[index], lambda at: arrived.at[at + 1])

    table[...] = jnp.zeros_like(table)
    embed_pad[...] = jnp.zeros_like(embed_pad)
    embed_pad[:, :33] = embed_weight[...]
    position = me * 1024 + lax.broadcasted_iota(jnp.int32, (16, 1024), 1)
    lag = jnp.where(me < 8, position, position - 16384)
    phase = ((lag * jnp.concatenate([bands[...]] * 8, axis=1)) & 16383).astype(jnp.float32)
    sines, cosines = sine_cosine(phase * (2.0 * math.pi / 16384))
    table[0:1, :] = lag[:1].astype(jnp.float32) * (1.0 / 8192)
    table[1:17, :] = sines
    table[17:33, :] = cosines
    wide = lambda columns: jnp.concatenate([columns] * 8, axis=1)
    bias = as_columns(jnp.concatenate([embed_bias[...]] * 2, axis=1))[:64]
    freq_rows = jnp.concatenate([frequency[...]] * 2, axis=1)
    freq_first, freq_second = as_columns(freq_rows[0:1])[:64], as_columns(freq_rows[1:2])[:64]
    before = exact_dot(embed_pad[...], table[...]) + wide(bias)
    pre_first[...] = before
    sine, cosine = sine_cosine(wide(freq_first) * before)
    sine_first[...] = sine
    cosine_first[...] = cosine
    before = exact_dot(hidden_weight[...], sine)
    pre_second[...] = before
    sine, cosine = sine_cosine(wide(freq_second) * before)
    sine_second[...] = sine
    cosine_second[...] = cosine
    decay_columns[...] = as_columns(decay_rate[...])
    weights = output_weight[pl.ds(pl.multiple_of(group * 64, 64), 64), :]
    decay = decay_columns[pl.ds(pl.multiple_of(group * 64, 64), 64), :]
    distance = jnp.abs(lag[:1]).astype(jnp.float32) * (1.0 / 8192)
    shape = jnp.exp(-wide(decay) * distance) * (1.0 / 128)
    window[...] = shape
    slope[...] = exact_dot(weights, sine) * shape * -distance

    cos_t, sin_t = twist[0], twist[1]

    def add_sequence(slot):
        parts = []
        for part in range(2):
            for channel in range(4):
                data = arrived[slot, channel, part]
                data = jnp.concatenate([data, data], axis=0)
                step = dot(first[...], data)
                real, imag = step[:64], step[64:]
                parts.append(
                    jnp.concatenate(
                        [real * cos_t - imag * sin_t, real * sin_t + imag * cos_t], axis=1
                    )
                )
        high, low = split_values(jnp.concatenate(parts, axis=0))
        whole = dot(jnp.concatenate([high, low, high], axis=1), forward[...])
        in_real, in_imag = whole[:256, :128], whole[:256, 128:]
        grad_real, grad_imag = whole[256:, :128], whole[256:, 128:]
        spectrum[:, :128] += in_real * grad_real + in_imag * grad_imag
        spectrum[:, 128:] += in_real * grad_imag - in_imag * grad_real

    own.wait()
    add_sequence(0)

    @pl.loop(0, 15)
    def _(at):
        pltpu.make_async_remote_copy(
            both.at[0],
            arrived.at[at + 1],
            dp_send.at[0, at],
            dp_recv.at[0, at],
            device_id={"y": y, "x": lax.rem(x + 1, 4)},
            device_id_type=MESH_ID,
        ).wait_recv()
        add_sequence(at + 1)

    high, low = split_values(spectrum[...])
    back = dot(jnp.concatenate([high, low, high], axis=1), backward[...])
    columns = []
    for channel in range(4):
        real = back[64 * channel : 64 * channel + 64, :128]
        imag = back[64 * channel : 64 * channel + 64, 128:]
        columns.append(
            jnp.concatenate([real * cos_t + imag * sin_t, imag * cos_t - real * sin_t], axis=0)
        )
    high, low = split_values(jnp.concatenate(columns, axis=1))
    result = dot(last[...], jnp.concatenate([high, low, high], axis=0))
    lags[...] = result.reshape(16, 8, 512)

    to_owner = over_dp(1, lambda index: lags.at[index], lambda at: mine.at[me])
    mine[me] = lags[me]
    for copy in to_owner:
        copy.wait_recv()
    for lag_row in range(8):
        for channel in range(4):
            rows[lag_row, pl.ds(channel, 16, stride=4), :] = mine[
                :, lag_row, 128 * channel : 128 * channel + 128
            ]
    to_row = over_chan(0, lambda index: rows.at[index], lambda at: landed.at[group])
    landed[group] = rows[group]

    lanes = ((1,), (1,))
    down = ((0,), (0,))
    ones = jnp.ones((8, 1024), jnp.float32)
    grad = jnp.concatenate([rows[lag_row] for lag_row in range(8)], axis=1)
    decay_row = exact_dot(ones, grad * slope[...], lanes)
    shaped = grad * window[...]
    output_grad = exact_dot(shaped, sine_second[...], lanes)
    turned = exact_dot(weights, shaped, down) * cosine_second[...]
    frequency_second = exact_dot(ones, turned * pre_second[...], lanes)
    turned = turned * wide(freq_second)
    hidden_grad = exact_dot(turned, sine_first[...], lanes)
    turned = exact_dot(hidden_weight[...], turned, down) * cosine_first[...]
    frequency_first = exact_dot(ones, turned * pre_first[...], lanes)
    turned = turned * wide(freq_first)
    bias_row = exact_dot(ones, turned, lanes)
    embed_grad = exact_dot(turned, table[...], lanes)

    shared = jnp.concatenate([hidden_grad, embed_grad[:, :64]], axis=1)
    for k in range(4):
        partial[:, k, :] = shared[16 * k : 16 * k + 16]
    packed = jnp.concatenate([output_grad[:32], output_grad[32:]], axis=1)
    for k in range(2):
        partial[:, 4 + k, :] = packed[16 * k : 16 * k + 16]
    vectors = jnp.concatenate([bias_row[:1], frequency_first[:1]], axis=1)
    partial[:, 6, :] = jnp.broadcast_to(vectors, (16, 128))
    vectors = jnp.concatenate([frequency_second[:1], decay_row[:1]], axis=1)
    partial[:, 7, :] = jnp.broadcast_to(vectors, (16, 128))
    to_sum = over_dp(2, lambda index: partial.at[index], lambda at: partials.at[me])
    partials[me] = partial[me]
    for copy in to_sum:
        copy.wait_recv()
    own_sum[...] = jnp.sum(partials[...], axis=0)
    to_groups = over_chan(1, lambda index: own_sum, lambda at: group_sums.at[group])
    group_sums[group] = own_sum[...]
    for copy in to_groups:
        copy.wait_recv()
    summed = jnp.sum(group_sums[...], axis=0)
    piece[0:4, :] = summed[0:4]
    piece[20:24, :] = jnp.zeros((4, 128), jnp.float32)
    for g in range(8):
        piece[4 + 2 * g : 6 + 2 * g, :] = group_sums[g, 4:6, :]
    to_all = over_dp(3, lambda index: piece, lambda at: pieces.at[me])
    pieces[me] = piece[...]
    bias_out[...] = summed[6:7, :64]
    frequency_out[0:1, :] = summed[6:7, 64:]
    frequency_out[1:2, :] = summed[7:8, :64]
    for g in range(8):
        decay_out[0:1, 64 * g : 64 * g + 64] = group_sums[g, 7:8, 64:]
    for copy in to_row:
        copy.wait_recv()
    filter_out[...] = landed[...].reshape(512, 128)
    for copy in to_all:
        copy.wait_recv()
    for k in range(4):
        block = pieces[:, k, :]
        hidden_out[16 * k : 16 * k + 16, :] = block[:, :64]
        embed_out[16 * k : 16 * k + 16, :] = block[:, 64:97]
    for g in range(8):
        for k in range(2):
            block = pieces[:, 4 + 2 * g + k, :]
            at = 64 * g + 16 * k
            output_out[at : at + 16, :] = block[:, :64]
            output_out[at + 32 : at + 48, :] = block[:, 64:]
    for copy in inputs + to_owner + to_row + to_sum + to_groups + to_all:
        copy.wait_send()


def local(
    signal,
    signal_grad,
    embed_weight,
    embed_bias,
    hidden_weight,
    frequency,
    output_weight,
    decay_rate,
):
    total = 2 * signal.shape[2]
    scale = 1.0 / math.sqrt(16 * signal.shape[2])
    both = jnp.stack(
        [signal.reshape(16, 4, 64, 128), signal_grad.reshape(16, 4, 64, 128)], axis=2
    )
    factors = [max(1, int(0.45 * total * 10000.0 ** (-band / 16))) for band in range(16)]
    bands = np.repeat(np.array(factors, np.int32)[:, None], 128, axis=1)
    tables = transform_tables(total, scale)
    vmem = pl.BlockSpec(memory_space=pltpu.VMEM)
    f32 = jnp.float32
    lags = pltpu.VMEM((64, 1024), f32)
    outs = pl.pallas_call(
        kernel,
        out_shape=[
            jax.ShapeDtypeStruct(shape, f32)
            for shape in [(512, 128), (64, 33), (1, 64), (64, 64), (2, 64), (512, 64), (1, 512)]
        ],
        in_specs=[pl.BlockSpec(memory_space=pl.ANY)] + [vmem] * 12,
        out_specs=[vmem] * 7,
        scratch_shapes=[
            pltpu.VMEM((16, 4, 2, 64, 128), jnp.bfloat16),
            pltpu.VMEM((256, 256), f32),
            pltpu.VMEM((16, 8, 512), f32),
            pltpu.VMEM((16, 8, 512), f32),
            pltpu.VMEM((8, 64, 128), f32),
            pltpu.VMEM((8, 64, 128), f32),
            pltpu.VMEM((128, 1024), f32),
            pltpu.VMEM((64, 128), f32),
            pltpu.VMEM((512, 128), f32),
            *[lags] * 8,
            pltpu.VMEM((16, 8, 128), f32),
            pltpu.VMEM((16, 8, 128), f32),
            pltpu.VMEM((8, 128), f32),
            pltpu.VMEM((8, 8, 128), f32),
            pltpu.VMEM((24, 128), f32),
            pltpu.VMEM((16, 24, 128), f32),
            pltpu.SemaphoreType.DMA,
            pltpu.SemaphoreType.DMA((4, 15)),
            pltpu.SemaphoreType.DMA((4, 15)),
            pltpu.SemaphoreType.DMA((2, 7)),
            pltpu.SemaphoreType.DMA((2, 7)),
        ],
        compiler_params=pltpu.CompilerParams(
            collective_id=0, has_side_effects=True, vmem_limit_bytes=40 * 1024 * 1024
        ),
    )(
        both,
        *[jnp.asarray(t) for t in tables],
        jnp.asarray(bands),
        embed_weight,
        embed_bias.reshape(1, 64),
        hidden_weight,
        frequency,
        output_weight,
        decay_rate.reshape(1, 512),
    )
    lag_grad, embed_grad, bias_grad, hidden_grad, frequency_grad, output_grad, decay_grad = outs
    return (
        lag_grad,
        embed_grad,
        bias_grad.reshape(64),
        hidden_grad,
        frequency_grad,
        output_grad,
        decay_grad.reshape(512),
    )


def solution(mesh):
    torus = Mesh(mesh.devices.reshape(4, 4, 4, 2), ("y", "x", "z", "core"))
    return jax.shard_map(
        local,
        mesh=torus,
        in_specs=(P(DP, CHAN, None), P(DP, CHAN, None), P(), P(), P(), P(), P(), P()),
        out_specs=(P(None, DP + CHAN), P(), P(), P(), P(), P(), P()),
        check_vma=False,
    )
```

```python
import math

import jax
import jax.numpy as jnp
import numpy as np
from jax import lax
from jax.experimental import pallas as pl
from jax.experimental.pallas import tpu as pltpu
from jax.sharding import Mesh
from jax.sharding import PartitionSpec as P

DP = ("y", "x")
CHAN = ("z", "core")
MESH_ID = pl.DeviceIdType.MESH
OFFSETS = sorted(
    [(dy, dx) for dy in range(4) for dx in range(4)],
    key=lambda p: (min(p[0], 4 - p[0]) + min(p[1], 4 - p[1])),
)
PEERS = sorted(
    [(dz, dc) for dz in range(4) for dc in range(2)], key=lambda p: (min(p[0], 4 - p[0]) + p[1])
)


def split_table(values):
    high = values.astype(jnp.bfloat16)
    low = (values - high.astype(np.float64)).astype(jnp.bfloat16)
    return high, low


def transform_tables(total, scale):
    half, side = 64, 128
    k1 = np.arange(half)[:, None] + 0.5
    n1 = np.arange(half)[None, :]
    angle = -2.0 * np.pi * k1 * n1 / side
    first = np.concatenate([np.cos(angle), np.sin(angle)], axis=0)
    first = np.concatenate(split_table(first), axis=1)
    n2 = np.arange(side)[None, :]
    angle = -2.0 * np.pi * k1 * n2 / total
    twist = np.stack([np.cos(angle), np.sin(angle)]).astype(np.float32)
    rows = np.arange(side)[:, None]
    angle = -2.0 * np.pi * (rows * n2 % side) / side
    cosine, sine = np.cos(angle), np.sin(angle)
    forward = np.block([[cosine, sine], [-sine, cosine]])
    high, low = split_table(forward)
    forward = np.concatenate([high, high, low], axis=0)
    backward = np.block([[cosine, -sine], [sine, cosine]])
    high, low = split_table(backward)
    backward = np.concatenate([high, high, low], axis=0)
    lag_row = np.arange(side)[:, None]
    freq = np.arange(half)[None, :] + 0.5
    angle = 2.0 * np.pi * lag_row * freq / side
    last = np.concatenate([np.cos(angle), -np.sin(angle)], axis=1)
    last = last * np.where(lag_row < half, 1.0, -1.0) * (2.0 * scale / total)
    high, low = split_table(last)
    last = np.concatenate([high, high, low], axis=1)
    return first, twist, forward, backward, last


def split_values(values):
    high = values.astype(jnp.bfloat16)
    low = (values - high.astype(jnp.float32)).astype(jnp.bfloat16)
    return high, low


def dot(a, b):
    return jnp.dot(a, b, preferred_element_type=jnp.float32)


def exact_dot(a, b, dims=((1,), (0,))):
    return lax.dot_general(
        a, b, (dims, ((), ())), precision=lax.Precision.HIGHEST, preferred_element_type=jnp.float32
    )


def sine_cosine(angle):
    turns = jnp.floor(angle * (2.0 / math.pi) + 0.5)
    rest = angle - turns * 1.5703125
    rest = rest - turns * 4.837512969970703125e-4
    rest = rest - turns * 7.54978995489188216e-8
    square = rest * rest
    sine = -1.9515295891e-4 * square + 8.3321608736e-3
    sine = sine * square - 1.6666654611e-1
    sine = sine * square * rest + rest
    cosine = 2.443315711809948e-5 * square - 1.388731625493765e-3
    cosine = cosine * square + 4.166664568298827e-2
    cosine = cosine * square * square - 0.5 * square + 1.0
    quarter = turns.astype(jnp.int32)
    odd = (quarter & 1) == 1
    first = jnp.where(odd, cosine, sine)
    second = jnp.where(odd, sine, cosine)
    first = jnp.where((quarter & 2) == 2, -first, first)
    second = jnp.where(((quarter + 1) & 2) == 2, -second, second)
    return first, second


def as_columns(row):
    return jnp.broadcast_to(row, (128, row.shape[1])).T


def kernel(
    signal,
    signal_grad,
    *refs,
):
    (
        *stored,
        landed,
        pieces,
        group_sums,
        first,
        twist,
        forward,
        backward,
        last,
        bands,
        embed_weight,
        embed_bias,
        hidden_weight,
        frequency,
        output_weight,
        decay_rate,
        natural,
        spread,
        both,
        arrived,
        spectrum,
        lags,
        mine,
        rows,
        table,
        embed_pad,
        decay_columns,
        output_rows,
        pre_first,
        sine_first,
        cosine_first,
        pre_second,
        sine_second,
        cosine_second,
        window,
        slope,
        partial,
        partials,
        own_sum,
        piece,
        local_sem,
        input_sem,
        table_sem,
        dp_send,
        dp_recv,
        chan_send,
        chan_recv,
    ) = refs
    y, x = lax.axis_index("y"), lax.axis_index("x")
    z, core = lax.axis_index("z"), lax.axis_index("core")
    me = y * 4 + x
    group = z * 2 + core

    barrier = pltpu.get_barrier_semaphore()
    dp_peers = []
    for dy, dx in OFFSETS[1:]:
        ty, tx = lax.rem(y + dy, 4), lax.rem(x + dx, 4)
        dp_peers.append((ty * 4 + tx, {"y": ty, "x": tx}))
    chan_peers = []
    for dz, dc in PEERS[1:]:
        tz, tc = lax.rem(z + dz, 4), lax.rem(core + dc, 2)
        chan_peers.append((tz * 2 + tc, {"z": tz, "core": tc}))
    for _, where in dp_peers[::-1] + chan_peers[::-1]:
        pl.semaphore_signal(barrier, 1, device_id=where, device_id_type=MESH_ID)
    loads = []
    for part, source in enumerate((signal, signal_grad)):
        loads.append(pltpu.make_async_copy(source, natural.at[part], input_sem.at[part]))
        loads[-1].start()
    fetches = []
    for at, source in enumerate(stored):
        fetches.append(pltpu.make_async_copy(source, refs[15 + at], table_sem.at[at]))
        fetches[-1].start()
    spectrum[...] = jnp.zeros_like(spectrum)

    for part in range(2):
        loads[part].wait()

        @pl.loop(0, 4)
        def _(block):
            for tile in range(64):
                piece_of = natural[
                    part, pl.ds(pl.multiple_of(block * 16, 16), 16), 128 * tile : 128 * tile + 128
                ]
                spread[pl.ds(tile, 16, stride=72), :] = piece_of.astype(jnp.float32)
            for peer in range(4):
                for channel in range(4):
                    at = 72 * (4 * peer + channel)
                    both[4 * block + peer, channel, part] = spread[at : at + 64, :].astype(
                        jnp.bfloat16
                    )

    own = pltpu.make_async_copy(both.at[me], arrived.at[0], local_sem)
    own.start()
    pl.semaphore_wait(barrier, len(dp_peers) + len(chan_peers))

    def exchange(stage, peers, sends, recvs, source, target, whole=False):
        copies = []
        order = list(enumerate(peers))
        for at, (index, where) in order if whole else order[::-1]:
            copy = pltpu.make_async_remote_copy(
                source(index),
                target(at),
                sends.at[stage, at],
                recvs.at[stage, at],
                device_id=where,
                device_id_type=MESH_ID,
            )
            copy.start()
            copies.append(copy)
        return copies

    over_dp = lambda stage, source, target: exchange(
        stage, dp_peers, dp_send, dp_recv, source, target, stage == 0
    )
    over_chan = lambda stage, source, target: exchange(
        stage, chan_peers, chan_send, chan_recv, source, target
    )

    inputs = over_dp(0, lambda index: both.at[index], lambda at: arrived.at[at + 1])

    for fetch in fetches:
        fetch.wait()

    table[...] = jnp.zeros_like(table)
    embed_pad[...] = jnp.zeros_like(embed_pad)
    embed_pad[:33, :] = embed_weight[...]
    position = me * 1024 + lax.broadcasted_iota(jnp.int32, (16, 1024), 1)
    lag = jnp.where(me < 8, position, position - 16384)
    phase = ((lag * jnp.concatenate([bands[...]] * 8, axis=1)) & 16383).astype(jnp.float32)
    sines, cosines = sine_cosine(phase * (2.0 * math.pi / 16384))
    table[0:1, :] = lag[:1].astype(jnp.float32) * (1.0 / 8192)
    table[1:17, :] = sines
    table[17:33, :] = cosines
    wide = lambda columns: jnp.concatenate([columns] * 8, axis=1)
    bias = as_columns(jnp.concatenate([embed_bias[...]] * 2, axis=1))[:64]
    freq_rows = jnp.concatenate([frequency[...]] * 2, axis=1)
    freq_first, freq_second = as_columns(freq_rows[0:1])[:64], as_columns(freq_rows[1:2])[:64]
    before = exact_dot(embed_pad[...], table[...], ((0,), (0,))) + wide(bias)
    pre_first[...] = before
    sine, cosine = sine_cosine(wide(freq_first) * before)
    sine_first[...] = sine
    cosine_first[...] = cosine
    before = exact_dot(hidden_weight[...], sine)
    pre_second[...] = before
    sine, cosine = sine_cosine(wide(freq_second) * before)
    sine_second[...] = sine
    cosine_second[...] = cosine
    decay_columns[...] = as_columns(decay_rate[...])
    output_rows[...] = output_weight[...].T
    weights = output_rows[pl.ds(pl.multiple_of(group * 64, 64), 64), :]
    decay = decay_columns[pl.ds(pl.multiple_of(group * 64, 64), 64), :]
    distance = jnp.abs(lag[:1]).astype(jnp.float32) * (1.0 / 8192)
    shape = jnp.exp(-wide(decay) * distance) * (1.0 / 128)
    window[...] = shape
    slope[...] = exact_dot(weights, sine) * shape * -distance

    cos_t, sin_t = twist[0], twist[1]

    def add_sequence(slot):
        parts = []
        for part in range(2):
            for channel in range(4):
                data = arrived[slot, channel, part]
                data = jnp.concatenate([data, data], axis=0)
                step = dot(first[...], data)
                real, imag = step[:64], step[64:]
                parts.append(
                    jnp.concatenate(
                        [real * cos_t - imag * sin_t, real * sin_t + imag * cos_t], axis=1
                    )
                )
        high, low = split_values(jnp.concatenate(parts, axis=0))
        whole = dot(jnp.concatenate([high, low, high], axis=1), forward[...])
        in_real, in_imag = whole[:256, :128], whole[:256, 128:]
        grad_real, grad_imag = whole[256:, :128], whole[256:, 128:]
        spectrum[:, :128] += in_real * grad_real + in_imag * grad_imag
        spectrum[:, 128:] += in_real * grad_imag - in_imag * grad_real

    own.wait()
    add_sequence(0)

    @pl.loop(0, 15)
    def _(at):
        pltpu.make_async_remote_copy(
            both.at[0],
            arrived.at[at + 1],
            dp_send.at[0, at],
            dp_recv.at[0, at],
            device_id={"y": y, "x": lax.rem(x + 1, 4)},
            device_id_type=MESH_ID,
        ).wait_recv()
        add_sequence(at + 1)

    high, low = split_values(spectrum[...])
    back = dot(jnp.concatenate([high, low, high], axis=1), backward[...])
    columns = []
    for channel in range(4):
        real = back[64 * channel : 64 * channel + 64, :128]
        imag = back[64 * channel : 64 * channel + 64, 128:]
        columns.append(
            jnp.concatenate([real * cos_t + imag * sin_t, imag * cos_t - real * sin_t], axis=0)
        )
    high, low = split_values(jnp.concatenate(columns, axis=1))
    result = dot(last[...], jnp.concatenate([high, low, high], axis=0))
    lags[...] = result.reshape(16, 8, 512)

    to_owner = over_dp(1, lambda index: lags.at[index], lambda at: mine.at[me])
    mine[me] = lags[me]
    for copy in to_owner:
        copy.wait_recv()
    for lag_row in range(8):
        for channel in range(4):
            rows[lag_row, pl.ds(channel, 16, stride=4), :] = mine[
                :, lag_row, 128 * channel : 128 * channel + 128
            ]
    to_row = over_chan(0, lambda index: rows.at[index], lambda at: landed.at[group])
    landed[group] = rows[group]

    lanes = ((1,), (1,))
    down = ((0,), (0,))
    ones = jnp.ones((8, 1024), jnp.float32)
    grad = jnp.concatenate([rows[lag_row] for lag_row in range(8)], axis=1)
    decay_row = exact_dot(ones, grad * slope[...], lanes)
    shaped = grad * window[...]
    output_grad = exact_dot(shaped, sine_second[...], lanes)
    turned = exact_dot(weights, shaped, down) * cosine_second[...]
    frequency_second = exact_dot(ones, turned * pre_second[...], lanes)
    turned = turned * wide(freq_second)
    hidden_grad = exact_dot(turned, sine_first[...], lanes)
    turned = exact_dot(hidden_weight[...], turned, down) * cosine_first[...]
    frequency_first = exact_dot(ones, turned * pre_first[...], lanes)
    turned = turned * wide(freq_first)
    bias_row = exact_dot(ones, turned, lanes)
    embed_grad = exact_dot(turned, table[...], lanes)

    shared = jnp.concatenate([hidden_grad, embed_grad[:, :64]], axis=1)
    for k in range(4):
        partial[:, k, :] = shared[16 * k : 16 * k + 16]
    packed = jnp.concatenate([output_grad[:32], output_grad[32:]], axis=1)
    for k in range(2):
        partial[:, 4 + k, :] = packed[16 * k : 16 * k + 16]
    vectors = jnp.concatenate([bias_row[:1], frequency_first[:1]], axis=1)
    partial[:, 6, :] = jnp.broadcast_to(vectors, (16, 128))
    vectors = jnp.concatenate([frequency_second[:1], decay_row[:1]], axis=1)
    partial[:, 7, :] = jnp.broadcast_to(vectors, (16, 128))
    to_sum = over_dp(2, lambda index: partial.at[index], lambda at: partials.at[me])
    partials[me] = partial[me]
    for copy in to_sum:
        copy.wait_recv()
    own_sum[...] = jnp.sum(partials[...], axis=0)
    to_groups = over_chan(1, lambda index: own_sum, lambda at: group_sums.at[group])
    group_sums[group] = own_sum[...]
    for copy in to_groups:
        copy.wait_recv()
    summed = jnp.sum(group_sums[...], axis=0)
    piece[0:4, :] = summed[0:4]
    piece[20:24, :] = jnp.zeros((4, 128), jnp.float32)
    for g in range(8):
        piece[4 + 2 * g : 6 + 2 * g, :] = group_sums[g, 4:6, :]
    to_all = over_dp(3, lambda index: piece, lambda at: pieces.at[me])
    pieces[me] = piece[...]
    for copy in to_row + to_all:
        copy.wait_recv()
    for copy in inputs + to_owner + to_row + to_sum + to_groups + to_all:
        copy.wait_send()


def finish(
    landed,
    pieces,
    group_sums,
    filter_out,
    embed_out,
    bias_out,
    hidden_out,
    frequency_out,
    output_out,
    decay_out,
    embed,
    bias,
    hidden,
    frequency,
    output_rows,
    output,
    decay,
    sems,
):
    copies = [pltpu.make_async_copy(landed, filter_out, sems.at[0])]
    copies[0].start()

    def send(source, target):
        copies.append(pltpu.make_async_copy(source, target, sems.at[len(copies)]))
        copies[-1].start()

    for g in range(8):
        for k in range(2):
            block = pieces[:, 4 + 2 * g + k, :]
            at = 64 * g + 16 * k
            output_rows[at : at + 16, :] = block[:, :64]
            output_rows[at + 32 : at + 48, :] = block[:, 64:]
    output[...] = output_rows[...].T
    send(output, output_out)
    rows = []
    for k in range(4):
        block = pieces[:, k, :]
        hidden[16 * k : 16 * k + 16, :] = block[:, :64]
        rows.append(block)
    send(hidden, hidden_out)
    embed[...] = jnp.concatenate(rows, axis=0).T[64:97]
    send(embed, embed_out)
    summed = jnp.sum(group_sums[:, 6:8, :], axis=0)
    bias[...] = summed[0:1, :64]
    send(bias, bias_out)
    frequency[0:1, :] = summed[0:1, 64:]
    frequency[1:2, :] = summed[1:2, :64]
    send(frequency, frequency_out)
    for g in range(8):
        decay[0:1, 64 * g : 64 * g + 64] = group_sums[g, 7:8, 64:]
    send(decay, decay_out)
    for copy in copies:
        copy.wait()


def local(
    signal,
    signal_grad,
    embed_weight,
    embed_bias,
    hidden_weight,
    frequency,
    output_weight,
    decay_rate,
):
    total = 2 * signal.shape[2]
    scale = 1.0 / math.sqrt(16 * signal.shape[2])
    factors = [max(1, int(0.45 * total * 10000.0 ** (-band / 16))) for band in range(16)]
    bands = np.repeat(np.array(factors, np.int32)[:, None], 128, axis=1)
    tables = transform_tables(total, scale)
    vmem = pl.BlockSpec(memory_space=pltpu.VMEM)
    f32 = jnp.float32
    lags = pltpu.VMEM((64, 1024), f32)
    stored = [jnp.asarray(t) for t in tables] + [
        jnp.asarray(bands),
        embed_weight.T,
        embed_bias.reshape(1, 64),
        hidden_weight,
        frequency,
        output_weight.T,
        decay_rate.reshape(1, 512),
    ]
    hbm = pl.BlockSpec(memory_space=pltpu.HBM)
    landed, pieces, group_sums = pl.pallas_call(
        kernel,
        out_shape=[
            jax.ShapeDtypeStruct(shape, f32) for shape in [(8, 64, 128), (16, 24, 128), (8, 8, 128)]
        ],
        in_specs=[hbm] * 14,
        out_specs=[vmem] * 3,
        scratch_shapes=[
            *[pltpu.VMEM(t.shape, t.dtype) for t in stored],
            pltpu.VMEM((2, 64, 8192), jnp.bfloat16),
            pltpu.VMEM((1152, 128), f32),
            pltpu.VMEM((16, 4, 2, 64, 128), jnp.bfloat16),
            pltpu.VMEM((16, 4, 2, 64, 128), jnp.bfloat16),
            pltpu.VMEM((256, 256), f32),
            pltpu.VMEM((16, 8, 512), f32),
            pltpu.VMEM((16, 8, 512), f32),
            pltpu.VMEM((8, 64, 128), f32),
            pltpu.VMEM((128, 1024), f32),
            pltpu.VMEM((128, 64), f32),
            pltpu.VMEM((512, 128), f32),
            pltpu.VMEM((512, 64), f32),
            *[lags] * 8,
            pltpu.VMEM((16, 8, 128), f32),
            pltpu.VMEM((16, 8, 128), f32),
            pltpu.VMEM((8, 128), f32),
            pltpu.VMEM((24, 128), f32),
            pltpu.SemaphoreType.DMA,
            pltpu.SemaphoreType.DMA((2,)),
            pltpu.SemaphoreType.DMA((12,)),
            pltpu.SemaphoreType.DMA((4, 15)),
            pltpu.SemaphoreType.DMA((4, 15)),
            pltpu.SemaphoreType.DMA((2, 7)),
            pltpu.SemaphoreType.DMA((2, 7)),
        ],
        compiler_params=pltpu.CompilerParams(
            collective_id=0, has_side_effects=True, vmem_limit_bytes=63 * 1024 * 1024
        ),
    )(signal[0], signal_grad[0], *stored)
    shapes = [(512, 128), (33, 64), (1, 64), (64, 64), (2, 64), (64, 512), (1, 512)]
    outs = pl.pallas_call(
        finish,
        out_shape=[jax.ShapeDtypeStruct(shape, f32) for shape in shapes],
        in_specs=[vmem] * 3,
        out_specs=[hbm] * 7,
        scratch_shapes=[
            *[pltpu.VMEM(shape, f32) for shape in shapes[1:5]],
            pltpu.VMEM((512, 64), f32),
            *[pltpu.VMEM(shape, f32) for shape in shapes[5:]],
            pltpu.SemaphoreType.DMA((7,)),
        ],
        compiler_params=pltpu.CompilerParams(vmem_limit_bytes=63 * 1024 * 1024),
    )(landed.reshape(512, 128), pieces, group_sums)
    lag_grad, embed_grad, bias_grad, hidden_grad, frequency_grad, output_grad, decay_grad = outs
    return (
        lag_grad,
        embed_grad.T,
        bias_grad.reshape(64),
        hidden_grad,
        frequency_grad,
        output_grad.T,
        decay_grad.reshape(512),
    )


def solution(mesh):
    torus = Mesh(mesh.devices.reshape(4, 4, 4, 2), ("y", "x", "z", "core"))
    return jax.shard_map(
        local,
        mesh=torus,
        in_specs=(P(DP, CHAN, None), P(DP, CHAN, None), P(), P(), P(), P(), P(), P()),
        out_specs=(P(None, DP + CHAN), P(), P(), P(), P(), P(), P()),
        check_vma=False,
    )
```

```python
import math

import jax
import jax.numpy as jnp
import numpy as np
from jax import lax
from jax.experimental import pallas as pl
from jax.experimental.pallas import tpu as pltpu
from jax.sharding import Mesh
from jax.sharding import PartitionSpec as P

DP = ("y", "x")
CHAN = ("z", "core")
MESH_ID = pl.DeviceIdType.MESH
OFFSETS = sorted(
    [(dy, dx) for dy in range(4) for dx in range(4)],
    key=lambda p: (min(p[0], 4 - p[0]) + min(p[1], 4 - p[1])),
)
PEERS = sorted(
    [(dz, dc) for dz in range(4) for dc in range(2)], key=lambda p: (min(p[0], 4 - p[0]) + p[1])
)


def split_table(values):
    high = values.astype(jnp.bfloat16)
    low = (values - high.astype(np.float64)).astype(jnp.bfloat16)
    return high, low


def transform_tables(total, scale):
    half, side = 64, 128
    k1 = np.arange(half)[:, None] + 0.5
    n1 = np.arange(half)[None, :]
    angle = -2.0 * np.pi * k1 * n1 / side
    first = np.concatenate([np.cos(angle), np.sin(angle)], axis=0)
    first = np.concatenate(split_table(first), axis=1)
    n2 = np.arange(side)[None, :]
    angle = -2.0 * np.pi * k1 * n2 / total
    twist = np.stack([np.cos(angle), np.sin(angle)]).astype(np.float32)
    rows = np.arange(side)[:, None]
    angle = -2.0 * np.pi * (rows * n2 % side) / side
    cosine, sine = np.cos(angle), np.sin(angle)
    forward = np.block([[cosine, sine], [-sine, cosine]])
    high, low = split_table(forward)
    forward = np.concatenate([high, high, low], axis=0)
    backward = np.block([[cosine, -sine], [sine, cosine]])
    high, low = split_table(backward)
    backward = np.concatenate([high, high, low], axis=0)
    lag_row = np.arange(side)[:, None]
    freq = np.arange(half)[None, :] + 0.5
    angle = 2.0 * np.pi * lag_row * freq / side
    last = np.concatenate([np.cos(angle), -np.sin(angle)], axis=1)
    last = last * np.where(lag_row < half, 1.0, -1.0) * (2.0 * scale / total)
    high, low = split_table(last)
    last = np.concatenate([high, high, low], axis=1)
    return first, twist, forward, backward, last


def split_values(values):
    high = values.astype(jnp.bfloat16)
    low = (values - high.astype(jnp.float32)).astype(jnp.bfloat16)
    return high, low


def dot(a, b):
    return jnp.dot(a, b, preferred_element_type=jnp.float32)


def exact_dot(a, b, dims=((1,), (0,))):
    return lax.dot_general(
        a, b, (dims, ((), ())), precision=lax.Precision.HIGHEST, preferred_element_type=jnp.float32
    )


def sine_cosine(angle):
    turns = jnp.floor(angle * (2.0 / math.pi) + 0.5)
    rest = angle - turns * 1.5703125
    rest = rest - turns * 4.837512969970703125e-4
    rest = rest - turns * 7.54978995489188216e-8
    square = rest * rest
    sine = -1.9515295891e-4 * square + 8.3321608736e-3
    sine = sine * square - 1.6666654611e-1
    sine = sine * square * rest + rest
    cosine = 2.443315711809948e-5 * square - 1.388731625493765e-3
    cosine = cosine * square + 4.166664568298827e-2
    cosine = cosine * square * square - 0.5 * square + 1.0
    quarter = turns.astype(jnp.int32)
    odd = (quarter & 1) == 1
    first = jnp.where(odd, cosine, sine)
    second = jnp.where(odd, sine, cosine)
    first = jnp.where((quarter & 2) == 2, -first, first)
    second = jnp.where(((quarter + 1) & 2) == 2, -second, second)
    return first, second


def as_columns(row):
    return jnp.broadcast_to(row, (128, row.shape[1])).T


def kernel(
    signal,
    signal_grad,
    *refs,
):
    (
        *stored,
        landed,
        pieces,
        group_sums,
        first,
        twist,
        forward,
        backward,
        last,
        bands,
        embed_weight,
        embed_bias,
        hidden_weight,
        frequency,
        output_weight,
        decay_rate,
        natural,
        spread,
        both,
        arrived,
        spectrum,
        lags,
        mine,
        rows,
        table,
        embed_pad,
        decay_columns,
        output_rows,
        pre_first,
        sine_first,
        cosine_first,
        pre_second,
        sine_second,
        cosine_second,
        window,
        slope,
        partial,
        partials,
        own_sum,
        piece,
        local_sem,
        input_sem,
        table_sem,
        arrive_sem,
        dp_send,
        dp_recv,
        chan_send,
        chan_recv,
    ) = refs
    y, x = lax.axis_index("y"), lax.axis_index("x")
    z, core = lax.axis_index("z"), lax.axis_index("core")
    me = y * 4 + x
    group = z * 2 + core

    barrier = pltpu.get_barrier_semaphore()
    dp_peers = []
    for dy, dx in OFFSETS[1:]:
        ty, tx = lax.rem(y + dy, 4), lax.rem(x + dx, 4)
        dp_peers.append((ty * 4 + tx, {"y": ty, "x": tx}))
    chan_peers = []
    for dz, dc in PEERS[1:]:
        tz, tc = lax.rem(z + dz, 4), lax.rem(core + dc, 2)
        chan_peers.append((tz * 2 + tc, {"z": tz, "core": tc}))
    for _, where in dp_peers[::-1] + chan_peers[::-1]:
        pl.semaphore_signal(barrier, 1, device_id=where, device_id_type=MESH_ID)
    loads = []
    for part, source in enumerate((signal, signal_grad)):
        loads.append(pltpu.make_async_copy(source, natural.at[part], input_sem.at[part]))
        loads[-1].start()
    fetches = []
    for at, source in enumerate(stored):
        fetches.append(pltpu.make_async_copy(source, refs[15 + at], table_sem.at[at]))
        fetches[-1].start()
    spectrum[...] = jnp.zeros_like(spectrum)

    for part in range(2):
        loads[part].wait()

        @pl.loop(0, 4)
        def _(block):
            for tile in range(64):
                piece_of = natural[
                    part, pl.ds(pl.multiple_of(block * 16, 16), 16), 128 * tile : 128 * tile + 128
                ]
                spread[pl.ds(tile, 16, stride=72), :] = piece_of.astype(jnp.float32)
            for peer in range(4):
                for channel in range(4):
                    at = 72 * (4 * peer + channel)
                    both[4 * block + peer, channel, part] = spread[at : at + 64, :].astype(
                        jnp.bfloat16
                    )

    own = pltpu.make_async_copy(both.at[me], arrived.at[0], local_sem)
    own.start()
    pl.semaphore_wait(barrier, len(dp_peers) + len(chan_peers))

    def exchange(peers, send, recvs, source, target, nearest=False):
        order = list(enumerate(peers))
        for at, (index, where) in order if nearest else order[::-1]:
            pltpu.make_async_remote_copy(
                source(index),
                target(at),
                send,
                recvs.at[at] if nearest else recvs,
                device_id=where,
                device_id_type=MESH_ID,
            ).start()

    def all_bytes(buffer, sem, count):
        part = buffer.at[pl.ds(0, count)]
        pltpu.make_async_copy(part, part, sem).wait()

    def over_dp(stage, source, target):
        exchange(dp_peers, dp_send.at[stage], dp_recv.at[stage], source, target)

    def over_chan(stage, source, target):
        exchange(chan_peers, chan_send.at[stage], chan_recv.at[stage], source, target)

    exchange(
        dp_peers,
        dp_send.at[0],
        arrive_sem,
        lambda index: both.at[index],
        lambda at: arrived.at[at + 1],
        nearest=True,
    )

    for fetch in fetches:
        fetch.wait()

    table[...] = jnp.zeros_like(table)
    embed_pad[...] = jnp.zeros_like(embed_pad)
    embed_pad[:33, :] = embed_weight[...]
    position = me * 1024 + lax.broadcasted_iota(jnp.int32, (16, 1024), 1)
    lag = jnp.where(me < 8, position, position - 16384)
    phase = ((lag * jnp.concatenate([bands[...]] * 8, axis=1)) & 16383).astype(jnp.float32)
    sines, cosines = sine_cosine(phase * (2.0 * math.pi / 16384))
    table[0:1, :] = lag[:1].astype(jnp.float32) * (1.0 / 8192)
    table[1:17, :] = sines
    table[17:33, :] = cosines
    wide = lambda columns: jnp.concatenate([columns] * 8, axis=1)
    bias = as_columns(jnp.concatenate([embed_bias[...]] * 2, axis=1))[:64]
    freq_rows = jnp.concatenate([frequency[...]] * 2, axis=1)
    freq_first, freq_second = as_columns(freq_rows[0:1])[:64], as_columns(freq_rows[1:2])[:64]
    before = exact_dot(embed_pad[...], table[...], ((0,), (0,))) + wide(bias)
    pre_first[...] = before
    sine, cosine = sine_cosine(wide(freq_first) * before)
    sine_first[...] = sine
    cosine_first[...] = cosine
    before = exact_dot(hidden_weight[...], sine)
    pre_second[...] = before
    sine, cosine = sine_cosine(wide(freq_second) * before)
    sine_second[...] = sine
    cosine_second[...] = cosine
    decay_columns[...] = as_columns(decay_rate[...])
    output_rows[...] = output_weight[...].T
    weights = output_rows[pl.ds(pl.multiple_of(group * 64, 64), 64), :]
    decay = decay_columns[pl.ds(pl.multiple_of(group * 64, 64), 64), :]
    distance = jnp.abs(lag[:1]).astype(jnp.float32) * (1.0 / 8192)
    shape = jnp.exp(-wide(decay) * distance) * (1.0 / 128)
    window[...] = shape
    slope[...] = exact_dot(weights, sine) * shape * -distance

    cos_t, sin_t = twist[0], twist[1]

    def add_sequence(slot):
        parts = []
        for part in range(2):
            for channel in range(4):
                data = arrived[slot, channel, part]
                data = jnp.concatenate([data, data], axis=0)
                step = dot(first[...], data)
                real, imag = step[:64], step[64:]
                parts.append(
                    jnp.concatenate(
                        [real * cos_t - imag * sin_t, real * sin_t + imag * cos_t], axis=1
                    )
                )
        high, low = split_values(jnp.concatenate(parts, axis=0))
        whole = dot(jnp.concatenate([high, low, high], axis=1), forward[...])
        in_real, in_imag = whole[:256, :128], whole[:256, 128:]
        grad_real, grad_imag = whole[256:, :128], whole[256:, 128:]
        spectrum[:, :128] += in_real * grad_real + in_imag * grad_imag
        spectrum[:, 128:] += in_real * grad_imag - in_imag * grad_real

    own.wait()
    add_sequence(0)

    @pl.loop(0, 15)
    def _(at):
        pltpu.make_async_remote_copy(
            both.at[0],
            arrived.at[at + 1],
            dp_send.at[0],
            arrive_sem.at[at],
            device_id={"y": y, "x": lax.rem(x + 1, 4)},
            device_id_type=MESH_ID,
        ).wait_recv()
        add_sequence(at + 1)

    high, low = split_values(spectrum[...])
    back = dot(jnp.concatenate([high, low, high], axis=1), backward[...])
    columns = []
    for channel in range(4):
        real = back[64 * channel : 64 * channel + 64, :128]
        imag = back[64 * channel : 64 * channel + 64, 128:]
        columns.append(
            jnp.concatenate([real * cos_t + imag * sin_t, imag * cos_t - real * sin_t], axis=0)
        )
    high, low = split_values(jnp.concatenate(columns, axis=1))
    result = dot(last[...], jnp.concatenate([high, low, high], axis=0))
    lags[...] = result.reshape(16, 8, 512)

    over_dp(1, lambda index: lags.at[index], lambda at: mine.at[me])
    mine[me] = lags[me]
    all_bytes(both, dp_send.at[0], 15)
    all_bytes(mine, dp_recv.at[1], 15)
    for lag_row in range(8):
        for channel in range(4):
            rows[lag_row, pl.ds(channel, 16, stride=4), :] = mine[
                :, lag_row, 128 * channel : 128 * channel + 128
            ]
    over_chan(0, lambda index: rows.at[index], lambda at: landed.at[group])
    landed[group] = rows[group]

    lanes = ((1,), (1,))
    down = ((0,), (0,))
    ones = jnp.ones((8, 1024), jnp.float32)
    grad = jnp.concatenate([rows[lag_row] for lag_row in range(8)], axis=1)
    decay_row = exact_dot(ones, grad * slope[...], lanes)
    shaped = grad * window[...]
    output_grad = exact_dot(shaped, sine_second[...], lanes)
    turned = exact_dot(weights, shaped, down) * cosine_second[...]
    frequency_second = exact_dot(ones, turned * pre_second[...], lanes)
    turned = turned * wide(freq_second)
    hidden_grad = exact_dot(turned, sine_first[...], lanes)
    turned = exact_dot(hidden_weight[...], turned, down) * cosine_first[...]
    frequency_first = exact_dot(ones, turned * pre_first[...], lanes)
    turned = turned * wide(freq_first)
    bias_row = exact_dot(ones, turned, lanes)
    embed_grad = exact_dot(turned, table[...], lanes)

    shared = jnp.concatenate([hidden_grad, embed_grad[:, :64]], axis=1)
    for k in range(4):
        partial[:, k, :] = shared[16 * k : 16 * k + 16]
    packed = jnp.concatenate([output_grad[:32], output_grad[32:]], axis=1)
    for k in range(2):
        partial[:, 4 + k, :] = packed[16 * k : 16 * k + 16]
    vectors = jnp.concatenate([bias_row[:1], frequency_first[:1]], axis=1)
    partial[:, 6, :] = jnp.broadcast_to(vectors, (16, 128))
    vectors = jnp.concatenate([frequency_second[:1], decay_row[:1]], axis=1)
    partial[:, 7, :] = jnp.broadcast_to(vectors, (16, 128))
    over_dp(2, lambda index: partial.at[index], lambda at: partials.at[me])
    partials[me] = partial[me]
    all_bytes(lags, dp_send.at[1], 15)
    all_bytes(rows, chan_send.at[0], 7)
    all_bytes(partials, dp_recv.at[2], 15)
    own_sum[...] = jnp.sum(partials[...], axis=0)
    over_chan(1, lambda index: own_sum, lambda at: group_sums.at[group])
    group_sums[group] = own_sum[...]
    all_bytes(group_sums, chan_recv.at[1], 7)
    summed = jnp.sum(group_sums[...], axis=0)
    piece[0:4, :] = summed[0:4]
    piece[20:24, :] = jnp.zeros((4, 128), jnp.float32)
    for g in range(8):
        piece[4 + 2 * g : 6 + 2 * g, :] = group_sums[g, 4:6, :]
    over_dp(3, lambda index: piece, lambda at: pieces.at[me])
    pieces[me] = piece[...]
    all_bytes(landed, chan_recv.at[0], 7)
    all_bytes(pieces, dp_recv.at[3], 15)
    all_bytes(partial, dp_send.at[2], 15)
    all_bytes(group_sums, chan_send.at[1], 7)
    all_bytes(pieces, dp_send.at[3], 15)


def finish(
    landed,
    pieces,
    group_sums,
    filter_out,
    embed_out,
    bias_out,
    hidden_out,
    frequency_out,
    output_out,
    decay_out,
    embed,
    bias,
    hidden,
    frequency,
    output_rows,
    output,
    decay,
    sems,
):
    copies = [pltpu.make_async_copy(landed, filter_out, sems.at[0])]
    copies[0].start()

    def send(source, target):
        copies.append(pltpu.make_async_copy(source, target, sems.at[len(copies)]))
        copies[-1].start()

    for g in range(8):
        for k in range(2):
            block = pieces[:, 4 + 2 * g + k, :]
            at = 64 * g + 16 * k
            output_rows[at : at + 16, :] = block[:, :64]
            output_rows[at + 32 : at + 48, :] = block[:, 64:]
    output[...] = output_rows[...].T
    send(output, output_out)
    rows = []
    for k in range(4):
        block = pieces[:, k, :]
        hidden[16 * k : 16 * k + 16, :] = block[:, :64]
        rows.append(block)
    send(hidden, hidden_out)
    embed[...] = jnp.concatenate(rows, axis=0).T[64:97]
    send(embed, embed_out)
    summed = jnp.sum(group_sums[:, 6:8, :], axis=0)
    bias[...] = summed[0:1, :64]
    send(bias, bias_out)
    frequency[0:1, :] = summed[0:1, 64:]
    frequency[1:2, :] = summed[1:2, :64]
    send(frequency, frequency_out)
    for g in range(8):
        decay[0:1, 64 * g : 64 * g + 64] = group_sums[g, 7:8, 64:]
    send(decay, decay_out)
    for copy in copies:
        copy.wait()


def local(
    signal,
    signal_grad,
    embed_weight,
    embed_bias,
    hidden_weight,
    frequency,
    output_weight,
    decay_rate,
):
    total = 2 * signal.shape[2]
    scale = 1.0 / math.sqrt(16 * signal.shape[2])
    factors = [max(1, int(0.45 * total * 10000.0 ** (-band / 16))) for band in range(16)]
    bands = np.repeat(np.array(factors, np.int32)[:, None], 128, axis=1)
    tables = transform_tables(total, scale)
    vmem = pl.BlockSpec(memory_space=pltpu.VMEM)
    f32 = jnp.float32
    lags = pltpu.VMEM((64, 1024), f32)
    stored = [jnp.asarray(t) for t in tables] + [
        jnp.asarray(bands),
        embed_weight.T,
        embed_bias.reshape(1, 64),
        hidden_weight,
        frequency,
        output_weight.T,
        decay_rate.reshape(1, 512),
    ]
    hbm = pl.BlockSpec(memory_space=pltpu.HBM)
    landed, pieces, group_sums = pl.pallas_call(
        kernel,
        out_shape=[
            jax.ShapeDtypeStruct(shape, f32) for shape in [(8, 64, 128), (16, 24, 128), (8, 8, 128)]
        ],
        in_specs=[hbm] * 14,
        out_specs=[vmem] * 3,
        scratch_shapes=[
            *[pltpu.VMEM(t.shape, t.dtype) for t in stored],
            pltpu.VMEM((2, 64, 8192), jnp.bfloat16),
            pltpu.VMEM((1152, 128), f32),
            pltpu.VMEM((16, 4, 2, 64, 128), jnp.bfloat16),
            pltpu.VMEM((16, 4, 2, 64, 128), jnp.bfloat16),
            pltpu.VMEM((256, 256), f32),
            pltpu.VMEM((16, 8, 512), f32),
            pltpu.VMEM((16, 8, 512), f32),
            pltpu.VMEM((8, 64, 128), f32),
            pltpu.VMEM((128, 1024), f32),
            pltpu.VMEM((128, 64), f32),
            pltpu.VMEM((512, 128), f32),
            pltpu.VMEM((512, 64), f32),
            *[lags] * 8,
            pltpu.VMEM((16, 8, 128), f32),
            pltpu.VMEM((16, 8, 128), f32),
            pltpu.VMEM((8, 128), f32),
            pltpu.VMEM((24, 128), f32),
            pltpu.SemaphoreType.DMA,
            pltpu.SemaphoreType.DMA((2,)),
            pltpu.SemaphoreType.DMA((12,)),
            pltpu.SemaphoreType.DMA((15,)),
            pltpu.SemaphoreType.DMA((4,)),
            pltpu.SemaphoreType.DMA((4,)),
            pltpu.SemaphoreType.DMA((2,)),
            pltpu.SemaphoreType.DMA((2,)),
        ],
        compiler_params=pltpu.CompilerParams(
            collective_id=0, has_side_effects=True, vmem_limit_bytes=40 * 1024 * 1024
        ),
    )(*[pltpu.with_memory_space_constraint(t, pltpu.HBM) for t in (signal[0], signal_grad[0], *stored)])
    shapes = [(512, 128), (33, 64), (1, 64), (64, 64), (2, 64), (64, 512), (1, 512)]
    outs = pl.pallas_call(
        finish,
        out_shape=[jax.ShapeDtypeStruct(shape, f32) for shape in shapes],
        in_specs=[vmem] * 3,
        out_specs=[hbm] * 7,
        scratch_shapes=[
            *[pltpu.VMEM(shape, f32) for shape in shapes[1:5]],
            pltpu.VMEM((512, 64), f32),
            *[pltpu.VMEM(shape, f32) for shape in shapes[5:]],
            pltpu.SemaphoreType.DMA((7,)),
        ],
        compiler_params=pltpu.CompilerParams(vmem_limit_bytes=8 * 1024 * 1024),
    )(landed.reshape(512, 128), pieces, group_sums)
    lag_grad, embed_grad, bias_grad, hidden_grad, frequency_grad, output_grad, decay_grad = outs
    return (
        lag_grad,
        embed_grad.T,
        bias_grad.reshape(64),
        hidden_grad,
        frequency_grad,
        output_grad.T,
        decay_grad.reshape(512),
    )


def solution(mesh):
    torus = Mesh(mesh.devices.reshape(4, 4, 4, 2), ("y", "x", "z", "core"))
    return jax.shard_map(
        local,
        mesh=torus,
        in_specs=(P(DP, CHAN, None), P(DP, CHAN, None), P(), P(), P(), P(), P(), P()),
        out_specs=(P(None, DP + CHAN), P(), P(), P(), P(), P(), P()),
        check_vma=False,
    )
```

```python
import math

import jax
import jax.numpy as jnp
import numpy as np
from jax import lax
from jax.experimental import pallas as pl
from jax.experimental.pallas import tpu as pltpu
from jax.sharding import Mesh
from jax.sharding import PartitionSpec as P

DP = ("y", "x")
CHAN = ("z", "core")
MESH_ID = pl.DeviceIdType.MESH
OFFSETS = sorted(
    [(dy, dx) for dy in range(4) for dx in range(4)],
    key=lambda p: (min(p[0], 4 - p[0]) + min(p[1], 4 - p[1])),
)
PEERS = sorted(
    [(dz, dc) for dz in range(4) for dc in range(2)], key=lambda p: (min(p[0], 4 - p[0]) + p[1])
)


def split_table(values):
    high = values.astype(jnp.bfloat16)
    low = (values - high.astype(np.float64)).astype(jnp.bfloat16)
    return high, low


def transform_tables(total, scale):
    half, side = 64, 128
    k1 = np.arange(half)[:, None] + 0.5
    n1 = np.arange(half)[None, :]
    angle = -2.0 * np.pi * k1 * n1 / side
    first = np.concatenate([np.cos(angle), np.sin(angle)], axis=0)
    first = np.concatenate(split_table(first), axis=1)
    n2 = np.arange(side)[None, :]
    angle = -2.0 * np.pi * k1 * n2 / total
    twist = np.stack([np.cos(angle), np.sin(angle)]).astype(np.float32)
    rows = np.arange(side)[:, None]
    angle = -2.0 * np.pi * (rows * n2 % side) / side
    cosine, sine = np.cos(angle), np.sin(angle)
    forward = np.block([[cosine, sine], [-sine, cosine]])
    high, low = split_table(forward)
    forward = np.concatenate([high, high, low], axis=0)
    backward = np.block([[cosine, -sine], [sine, cosine]])
    high, low = split_table(backward)
    backward = np.concatenate([high, high, low], axis=0)
    lag_row = np.arange(side)[:, None]
    freq = np.arange(half)[None, :] + 0.5
    angle = 2.0 * np.pi * lag_row * freq / side
    last = np.concatenate([np.cos(angle), -np.sin(angle)], axis=1)
    last = last * np.where(lag_row < half, 1.0, -1.0) * (2.0 * scale / total)
    high, low = split_table(last)
    last = np.concatenate([high, high, low], axis=1)
    return first, twist, forward, backward, last


def split_values(values):
    high = values.astype(jnp.bfloat16)
    low = (values - high.astype(jnp.float32)).astype(jnp.bfloat16)
    return high, low


def dot(a, b):
    return jnp.dot(a, b, preferred_element_type=jnp.float32)


def exact_dot(a, b, dims=((1,), (0,))):
    return lax.dot_general(
        a, b, (dims, ((), ())), precision=lax.Precision.HIGHEST, preferred_element_type=jnp.float32
    )


def sine_cosine(angle):
    turns = jnp.floor(angle * (2.0 / math.pi) + 0.5)
    rest = angle - turns * 1.5703125
    rest = rest - turns * 4.837512969970703125e-4
    rest = rest - turns * 7.54978995489188216e-8
    square = rest * rest
    sine = -1.9515295891e-4 * square + 8.3321608736e-3
    sine = sine * square - 1.6666654611e-1
    sine = sine * square * rest + rest
    cosine = 2.443315711809948e-5 * square - 1.388731625493765e-3
    cosine = cosine * square + 4.166664568298827e-2
    cosine = cosine * square * square - 0.5 * square + 1.0
    quarter = turns.astype(jnp.int32)
    odd = (quarter & 1) == 1
    first = jnp.where(odd, cosine, sine)
    second = jnp.where(odd, sine, cosine)
    first = jnp.where((quarter & 2) == 2, -first, first)
    second = jnp.where(((quarter + 1) & 2) == 2, -second, second)
    return first, second


def as_columns(row):
    return jnp.broadcast_to(row, (128, row.shape[1])).T


def kernel(
    signal,
    signal_grad,
    *refs,
):
    (
        *stored,
        landed,
        pieces,
        group_sums,
        first,
        twist,
        forward,
        backward,
        last,
        bands,
        embed_weight,
        embed_bias,
        hidden_weight,
        frequency,
        output_weight,
        decay_rate,
        natural,
        spread,
        both,
        arrived,
        spectrum,
        lags,
        mine,
        rows,
        table,
        embed_pad,
        decay_columns,
        output_rows,
        pre_first,
        sine_first,
        cosine_first,
        pre_second,
        sine_second,
        cosine_second,
        window,
        slope,
        partial,
        partials,
        own_sum,
        piece,
        local_sem,
        input_sem,
        table_sem,
        entered,
        arrive_sem,
        dp_send,
        dp_recv,
        chan_send,
        chan_recv,
    ) = refs
    y, x = lax.axis_index("y"), lax.axis_index("x")
    z, core = lax.axis_index("z"), lax.axis_index("core")
    me = y * 4 + x
    group = z * 2 + core

    barrier = pltpu.get_barrier_semaphore()
    dp_peers = []
    for dy, dx in OFFSETS[1:]:
        ty, tx = lax.rem(y + dy, 4), lax.rem(x + dx, 4)
        dp_peers.append((ty * 4 + tx, {"y": ty, "x": tx}))
    chan_peers = []
    for dz, dc in PEERS[1:]:
        tz, tc = lax.rem(z + dz, 4), lax.rem(core + dc, 2)
        chan_peers.append((tz * 2 + tc, {"z": tz, "core": tc}))
    neighbours = [where for _, where in dp_peers[:4] + chan_peers[:3]]

    def greet(sem):
        for where in neighbours:
            pl.semaphore_signal(sem, 1, device_id=where, device_id_type=MESH_ID)

    greet(barrier)
    loads = []
    for part, source in enumerate((signal, signal_grad)):
        loads.append(pltpu.make_async_copy(source, natural.at[part], input_sem.at[part]))
        loads[-1].start()
    fetches = []
    for at, source in enumerate(stored):
        fetches.append(pltpu.make_async_copy(source, refs[15 + at], table_sem.at[at]))
        fetches[-1].start()
    spectrum[...] = jnp.zeros_like(spectrum)

    for part in range(2):
        loads[part].wait()
        if part == 1:
            pl.semaphore_wait(barrier, 7)
            greet(entered.at[0])

        @pl.loop(0, 4)
        def _(block):
            for tile in range(64):
                piece_of = natural[
                    part, pl.ds(pl.multiple_of(block * 16, 16), 16), 128 * tile : 128 * tile + 128
                ]
                spread[pl.ds(tile, 16, stride=72), :] = piece_of.astype(jnp.float32)
            for peer in range(4):
                for channel in range(4):
                    at = 72 * (4 * peer + channel)
                    both[4 * block + peer, channel, part] = spread[at : at + 64, :].astype(
                        jnp.bfloat16
                    )

    own = pltpu.make_async_copy(both.at[me], arrived.at[0], local_sem)
    own.start()

    def exchange(peers, send, recvs, source, target, nearest=False):
        order = peers if nearest else list(enumerate(peers))
        for at, (index, where) in order if nearest else order[::-1]:
            pltpu.make_async_remote_copy(
                source(index),
                target(at),
                send,
                recvs.at[at] if nearest else recvs,
                device_id=where,
                device_id_type=MESH_ID,
            ).start()

    def all_bytes(buffer, sem, count):
        part = buffer.at[pl.ds(0, count)]
        pltpu.make_async_copy(part, part, sem).wait()

    def over_dp(stage, source, target):
        exchange(dp_peers, dp_send.at[stage], dp_recv.at[stage], source, target)

    def over_chan(stage, source, target):
        exchange(chan_peers, chan_send.at[stage], chan_recv.at[stage], source, target)

    def send_inputs(first_peer, last_peer):
        exchange(
            list(enumerate(dp_peers))[first_peer:last_peer],
            dp_send.at[0],
            arrive_sem,
            lambda index: both.at[index],
            lambda at: arrived.at[at + 1],
            nearest=True,
        )

    send_inputs(0, 4)
    for fetch in fetches:
        fetch.wait()

    table[...] = jnp.zeros_like(table)
    embed_pad[...] = jnp.zeros_like(embed_pad)
    embed_pad[:33, :] = embed_weight[...]
    position = me * 1024 + lax.broadcasted_iota(jnp.int32, (16, 1024), 1)
    lag = jnp.where(me < 8, position, position - 16384)
    phase = ((lag * jnp.concatenate([bands[...]] * 8, axis=1)) & 16383).astype(jnp.float32)
    sines, cosines = sine_cosine(phase * (2.0 * math.pi / 16384))
    table[0:1, :] = lag[:1].astype(jnp.float32) * (1.0 / 8192)
    table[1:17, :] = sines
    table[17:33, :] = cosines
    pl.semaphore_wait(entered.at[0], 7)
    greet(entered.at[1])
    send_inputs(4, 10)
    wide = lambda columns: jnp.concatenate([columns] * 8, axis=1)
    bias = as_columns(jnp.concatenate([embed_bias[...]] * 2, axis=1))[:64]
    freq_rows = jnp.concatenate([frequency[...]] * 2, axis=1)
    freq_first, freq_second = as_columns(freq_rows[0:1])[:64], as_columns(freq_rows[1:2])[:64]
    before = exact_dot(embed_pad[...], table[...], ((0,), (0,))) + wide(bias)
    pre_first[...] = before
    sine, cosine = sine_cosine(wide(freq_first) * before)
    sine_first[...] = sine
    cosine_first[...] = cosine
    pl.semaphore_wait(entered.at[1], 7)
    greet(entered.at[2])
    send_inputs(10, 14)
    before = exact_dot(hidden_weight[...], sine)
    pre_second[...] = before
    sine, cosine = sine_cosine(wide(freq_second) * before)
    sine_second[...] = sine
    cosine_second[...] = cosine
    decay_columns[...] = as_columns(decay_rate[...])
    output_rows[...] = output_weight[...].T
    weights = output_rows[pl.ds(pl.multiple_of(group * 64, 64), 64), :]
    decay = decay_columns[pl.ds(pl.multiple_of(group * 64, 64), 64), :]
    distance = jnp.abs(lag[:1]).astype(jnp.float32) * (1.0 / 8192)
    shape = jnp.exp(-wide(decay) * distance) * (1.0 / 128)
    window[...] = shape
    slope[...] = exact_dot(weights, sine) * shape * -distance

    cos_t, sin_t = twist[0], twist[1]

    def add_sequence(slot):
        parts = []
        for part in range(2):
            for channel in range(4):
                data = arrived[slot, channel, part]
                data = jnp.concatenate([data, data], axis=0)
                step = dot(first[...], data)
                real, imag = step[:64], step[64:]
                parts.append(
                    jnp.concatenate(
                        [real * cos_t - imag * sin_t, real * sin_t + imag * cos_t], axis=1
                    )
                )
        high, low = split_values(jnp.concatenate(parts, axis=0))
        whole = dot(jnp.concatenate([high, low, high], axis=1), forward[...])
        in_real, in_imag = whole[:256, :128], whole[:256, 128:]
        grad_real, grad_imag = whole[256:, :128], whole[256:, 128:]
        spectrum[:, :128] += in_real * grad_real + in_imag * grad_imag
        spectrum[:, 128:] += in_real * grad_imag - in_imag * grad_real

    pl.semaphore_wait(entered.at[2], 7)
    send_inputs(14, 15)
    own.wait()
    add_sequence(0)

    @pl.loop(0, 15)
    def _(at):
        pltpu.make_async_remote_copy(
            both.at[0],
            arrived.at[at + 1],
            dp_send.at[0],
            arrive_sem.at[at],
            device_id={"y": y, "x": lax.rem(x + 1, 4)},
            device_id_type=MESH_ID,
        ).wait_recv()
        add_sequence(at + 1)

    high, low = split_values(spectrum[...])
    back = dot(jnp.concatenate([high, low, high], axis=1), backward[...])
    columns = []
    for channel in range(4):
        real = back[64 * channel : 64 * channel + 64, :128]
        imag = back[64 * channel : 64 * channel + 64, 128:]
        columns.append(
            jnp.concatenate([real * cos_t + imag * sin_t, imag * cos_t - real * sin_t], axis=0)
        )
    high, low = split_values(jnp.concatenate(columns, axis=1))
    result = dot(last[...], jnp.concatenate([high, low, high], axis=0))
    lags[...] = result.reshape(16, 8, 512)

    over_dp(1, lambda index: lags.at[index], lambda at: mine.at[me])
    mine[me] = lags[me]
    all_bytes(both, dp_send.at[0], 15)
    all_bytes(mine, dp_recv.at[1], 15)
    for lag_row in range(8):
        for channel in range(4):
            rows[lag_row, pl.ds(channel, 16, stride=4), :] = mine[
                :, lag_row, 128 * channel : 128 * channel + 128
            ]
    over_chan(0, lambda index: rows.at[index], lambda at: landed.at[group])
    landed[group] = rows[group]

    lanes = ((1,), (1,))
    down = ((0,), (0,))
    ones = jnp.ones((8, 1024), jnp.float32)
    grad = jnp.concatenate([rows[lag_row] for lag_row in range(8)], axis=1)
    decay_row = exact_dot(ones, grad * slope[...], lanes)
    shaped = grad * window[...]
    output_grad = exact_dot(shaped, sine_second[...], lanes)
    turned = exact_dot(weights, shaped, down) * cosine_second[...]
    frequency_second = exact_dot(ones, turned * pre_second[...], lanes)
    turned = turned * wide(freq_second)
    hidden_grad = exact_dot(turned, sine_first[...], lanes)
    turned = exact_dot(hidden_weight[...], turned, down) * cosine_first[...]
    frequency_first = exact_dot(ones, turned * pre_first[...], lanes)
    turned = turned * wide(freq_first)
    bias_row = exact_dot(ones, turned, lanes)
    embed_grad = exact_dot(turned, table[...], lanes)

    shared = jnp.concatenate([hidden_grad, embed_grad[:, :64]], axis=1)
    for k in range(4):
        partial[:, k, :] = shared[16 * k : 16 * k + 16]
    packed = jnp.concatenate([output_grad[:32], output_grad[32:]], axis=1)
    for k in range(2):
        partial[:, 4 + k, :] = packed[16 * k : 16 * k + 16]
    vectors = jnp.concatenate([bias_row[:1], frequency_first[:1]], axis=1)
    partial[:, 6, :] = jnp.broadcast_to(vectors, (16, 128))
    vectors = jnp.concatenate([frequency_second[:1], decay_row[:1]], axis=1)
    partial[:, 7, :] = jnp.broadcast_to(vectors, (16, 128))
    over_dp(2, lambda index: partial.at[index], lambda at: partials.at[me])
    partials[me] = partial[me]
    all_bytes(lags, dp_send.at[1], 15)
    all_bytes(rows, chan_send.at[0], 7)
    all_bytes(partials, dp_recv.at[2], 15)
    own_sum[...] = jnp.sum(partials[...], axis=0)
    over_chan(1, lambda index: own_sum, lambda at: group_sums.at[group])
    group_sums[group] = own_sum[...]
    all_bytes(group_sums, chan_recv.at[1], 7)
    summed = jnp.sum(group_sums[...], axis=0)
    piece[0:4, :] = summed[0:4]
    piece[20:24, :] = jnp.zeros((4, 128), jnp.float32)
    for g in range(8):
        piece[4 + 2 * g : 6 + 2 * g, :] = group_sums[g, 4:6, :]
    over_dp(3, lambda index: piece, lambda at: pieces.at[me])
    pieces[me] = piece[...]
    all_bytes(landed, chan_recv.at[0], 7)
    all_bytes(pieces, dp_recv.at[3], 15)
    all_bytes(partial, dp_send.at[2], 15)
    all_bytes(group_sums, chan_send.at[1], 7)
    all_bytes(pieces, dp_send.at[3], 15)


def finish(
    landed,
    pieces,
    group_sums,
    filter_out,
    embed_out,
    bias_out,
    hidden_out,
    frequency_out,
    output_out,
    decay_out,
    embed,
    bias,
    hidden,
    frequency,
    output_rows,
    output,
    decay,
    sems,
):
    copies = [pltpu.make_async_copy(landed, filter_out, sems.at[0])]
    copies[0].start()

    def send(source, target):
        copies.append(pltpu.make_async_copy(source, target, sems.at[len(copies)]))
        copies[-1].start()

    for g in range(8):
        for k in range(2):
            block = pieces[:, 4 + 2 * g + k, :]
            at = 64 * g + 16 * k
            output_rows[at : at + 16, :] = block[:, :64]
            output_rows[at + 32 : at + 48, :] = block[:, 64:]
    output[...] = output_rows[...].T
    send(output, output_out)
    rows = []
    for k in range(4):
        block = pieces[:, k, :]
        hidden[16 * k : 16 * k + 16, :] = block[:, :64]
        rows.append(block)
    send(hidden, hidden_out)
    embed[...] = jnp.concatenate(rows, axis=0).T[64:97]
    send(embed, embed_out)
    summed = jnp.sum(group_sums[:, 6:8, :], axis=0)
    bias[...] = summed[0:1, :64]
    send(bias, bias_out)
    frequency[0:1, :] = summed[0:1, 64:]
    frequency[1:2, :] = summed[1:2, :64]
    send(frequency, frequency_out)
    for g in range(8):
        decay[0:1, 64 * g : 64 * g + 64] = group_sums[g, 7:8, 64:]
    send(decay, decay_out)
    for copy in copies:
        copy.wait()


def local(
    signal,
    signal_grad,
    embed_weight,
    embed_bias,
    hidden_weight,
    frequency,
    output_weight,
    decay_rate,
):
    total = 2 * signal.shape[2]
    scale = 1.0 / math.sqrt(16 * signal.shape[2])
    factors = [max(1, int(0.45 * total * 10000.0 ** (-band / 16))) for band in range(16)]
    bands = np.repeat(np.array(factors, np.int32)[:, None], 128, axis=1)
    tables = transform_tables(total, scale)
    vmem = pl.BlockSpec(memory_space=pltpu.VMEM)
    f32 = jnp.float32
    lags = pltpu.VMEM((64, 1024), f32)
    stored = [jnp.asarray(t) for t in tables] + [
        jnp.asarray(bands),
        embed_weight.T,
        embed_bias.reshape(1, 64),
        hidden_weight,
        frequency,
        output_weight.T,
        decay_rate.reshape(1, 512),
    ]
    hbm = pl.BlockSpec(memory_space=pltpu.HBM)
    landed, pieces, group_sums = pl.pallas_call(
        kernel,
        out_shape=[
            jax.ShapeDtypeStruct(shape, f32) for shape in [(8, 64, 128), (16, 24, 128), (8, 8, 128)]
        ],
        in_specs=[hbm] * 14,
        out_specs=[vmem] * 3,
        scratch_shapes=[
            *[pltpu.VMEM(t.shape, t.dtype) for t in stored],
            pltpu.VMEM((2, 64, 8192), jnp.bfloat16),
            pltpu.VMEM((1152, 128), f32),
            pltpu.VMEM((16, 4, 2, 64, 128), jnp.bfloat16),
            pltpu.VMEM((16, 4, 2, 64, 128), jnp.bfloat16),
            pltpu.VMEM((256, 256), f32),
            pltpu.VMEM((16, 8, 512), f32),
            pltpu.VMEM((16, 8, 512), f32),
            pltpu.VMEM((8, 64, 128), f32),
            pltpu.VMEM((128, 1024), f32),
            pltpu.VMEM((128, 64), f32),
            pltpu.VMEM((512, 128), f32),
            pltpu.VMEM((512, 64), f32),
            *[lags] * 8,
            pltpu.VMEM((16, 8, 128), f32),
            pltpu.VMEM((16, 8, 128), f32),
            pltpu.VMEM((8, 128), f32),
            pltpu.VMEM((24, 128), f32),
            pltpu.SemaphoreType.DMA,
            pltpu.SemaphoreType.DMA((2,)),
            pltpu.SemaphoreType.DMA((12,)),
            pltpu.SemaphoreType.REGULAR((3,)),
            pltpu.SemaphoreType.DMA((15,)),
            pltpu.SemaphoreType.DMA((4,)),
            pltpu.SemaphoreType.DMA((4,)),
            pltpu.SemaphoreType.DMA((2,)),
            pltpu.SemaphoreType.DMA((2,)),
        ],
        compiler_params=pltpu.CompilerParams(
            collective_id=0, has_side_effects=True, vmem_limit_bytes=40 * 1024 * 1024
        ),
    )(*[pltpu.with_memory_space_constraint(t, pltpu.HBM) for t in (signal[0], signal_grad[0], *stored)])
    shapes = [(512, 128), (33, 64), (1, 64), (64, 64), (2, 64), (64, 512), (1, 512)]
    outs = pl.pallas_call(
        finish,
        out_shape=[jax.ShapeDtypeStruct(shape, f32) for shape in shapes],
        in_specs=[vmem] * 3,
        out_specs=[hbm] * 7,
        scratch_shapes=[
            *[pltpu.VMEM(shape, f32) for shape in shapes[1:5]],
            pltpu.VMEM((512, 64), f32),
            *[pltpu.VMEM(shape, f32) for shape in shapes[5:]],
            pltpu.SemaphoreType.DMA((7,)),
        ],
        compiler_params=pltpu.CompilerParams(vmem_limit_bytes=8 * 1024 * 1024),
    )(landed.reshape(512, 128), pieces, group_sums)
    lag_grad, embed_grad, bias_grad, hidden_grad, frequency_grad, output_grad, decay_grad = outs
    return (
        lag_grad,
        embed_grad.T,
        bias_grad.reshape(64),
        hidden_grad,
        frequency_grad,
        output_grad.T,
        decay_grad.reshape(512),
    )


def solution(mesh):
    torus = Mesh(mesh.devices.reshape(4, 4, 4, 2), ("y", "x", "z", "core"))
    return jax.shard_map(
        local,
        mesh=torus,
        in_specs=(P(DP, CHAN, None), P(DP, CHAN, None), P(), P(), P(), P(), P(), P()),
        out_specs=(P(None, DP + CHAN), P(), P(), P(), P(), P(), P()),
        check_vma=False,
    )
```

```python
import math

import jax
import jax.numpy as jnp
import numpy as np
from jax import lax
from jax.experimental import pallas as pl
from jax.experimental.pallas import tpu as pltpu
from jax.sharding import Mesh
from jax.sharding import PartitionSpec as P

DP = ("y", "x")
CHAN = ("z", "core")
MESH_ID = pl.DeviceIdType.MESH
OFFSETS = sorted(
    [(dy, dx) for dy in range(4) for dx in range(4)],
    key=lambda p: (min(p[0], 4 - p[0]) + min(p[1], 4 - p[1])),
)
PEERS = sorted(
    [(dz, dc) for dz in range(4) for dc in range(2)], key=lambda p: (min(p[0], 4 - p[0]) + p[1])
)


def split_table(values):
    high = values.astype(jnp.bfloat16)
    low = (values - high.astype(np.float64)).astype(jnp.bfloat16)
    return high, low


def transform_tables(total, scale):
    half, side = 64, 128
    k1 = np.arange(half)[:, None] + 0.5
    n1 = np.arange(half)[None, :]
    angle = -2.0 * np.pi * k1 * n1 / side
    first = np.concatenate([np.cos(angle), np.sin(angle)], axis=0)
    first = np.concatenate(split_table(first), axis=1)
    n2 = np.arange(side)[None, :]
    angle = -2.0 * np.pi * k1 * n2 / total
    twist = np.stack([np.cos(angle), np.sin(angle)]).astype(np.float32)
    rows = np.arange(side)[:, None]
    angle = -2.0 * np.pi * (rows * n2 % side) / side
    cosine, sine = np.cos(angle), np.sin(angle)
    forward = np.block([[cosine, sine], [-sine, cosine]])
    high, low = split_table(forward)
    forward = np.concatenate([high, high, low], axis=0)
    backward = np.block([[cosine, -sine], [sine, cosine]])
    high, low = split_table(backward)
    backward = np.concatenate([high, high, low], axis=0)
    lag_row = np.arange(side)[:, None]
    freq = np.arange(half)[None, :] + 0.5
    angle = 2.0 * np.pi * lag_row * freq / side
    last = np.concatenate([np.cos(angle), -np.sin(angle)], axis=1)
    last = last * np.where(lag_row < half, 1.0, -1.0) * (2.0 * scale / total)
    high, low = split_table(last)
    last = np.concatenate([high, high, low], axis=1)
    return first, twist, forward, backward, last


def split_values(values):
    high = values.astype(jnp.bfloat16)
    low = (values - high.astype(jnp.float32)).astype(jnp.bfloat16)
    return high, low


def dot(a, b):
    return jnp.dot(a, b, preferred_element_type=jnp.float32)


def lane_dot(a, b):
    return lax.dot_general(a, b, (((1,), (1,)), ((), ())), preferred_element_type=jnp.float32)


def kept(values):
    high, low = split_values(values)
    return jnp.concatenate([high, high, low], axis=1)


def met(high, low, axis):
    return jnp.concatenate([high, low, high], axis=axis)


def exact_dot(a, b, dims=((1,), (0,))):
    return lax.dot_general(
        a, b, (dims, ((), ())), precision=lax.Precision.HIGHEST, preferred_element_type=jnp.float32
    )


def sine_cosine(angle):
    turns = jnp.floor(angle * (2.0 / math.pi) + 0.5)
    rest = angle - turns * 1.5703125
    rest = rest - turns * 4.837512969970703125e-4
    rest = rest - turns * 7.54978995489188216e-8
    square = rest * rest
    sine = -1.9515295891e-4 * square + 8.3321608736e-3
    sine = sine * square - 1.6666654611e-1
    sine = sine * square * rest + rest
    cosine = 2.443315711809948e-5 * square - 1.388731625493765e-3
    cosine = cosine * square + 4.166664568298827e-2
    cosine = cosine * square * square - 0.5 * square + 1.0
    quarter = turns.astype(jnp.int32)
    odd = (quarter & 1) == 1
    first = jnp.where(odd, cosine, sine)
    second = jnp.where(odd, sine, cosine)
    first = jnp.where((quarter & 2) == 2, -first, first)
    second = jnp.where(((quarter + 1) & 2) == 2, -second, second)
    return first, second


def as_columns(row):
    return jnp.broadcast_to(row, (128, row.shape[1])).T


def kernel(
    signal,
    signal_grad,
    *refs,
):
    (
        *stored,
        landed,
        pieces,
        group_sums,
        used,
        first,
        twist,
        forward,
        backward,
        last,
        bands,
        embed_weight,
        embed_bias,
        hidden_weight,
        frequency,
        output_weight,
        decay_rate,
        natural,
        spread,
        both,
        arrived,
        spectrum,
        lags,
        mine,
        rows,
        table,
        table_kept,
        weights_kept,
        hidden_kept,
        embed_pad,
        decay_columns,
        output_rows,
        sine_first,
        cosine_first,
        sine_second,
        cosine_second,
        window,
        slope,
        partial,
        partials,
        own_sum,
        piece,
        local_sem,
        input_sem,
        table_sem,
        entered,
        arrive_sem,
        dp_send,
        dp_recv,
        chan_send,
        chan_recv,
    ) = refs
    y, x = lax.axis_index("y"), lax.axis_index("x")
    z, core = lax.axis_index("z"), lax.axis_index("core")
    me = y * 4 + x
    group = z * 2 + core

    barrier = pltpu.get_barrier_semaphore()
    dp_peers = []
    for dy, dx in OFFSETS[1:]:
        ty, tx = lax.rem(y + dy, 4), lax.rem(x + dx, 4)
        dp_peers.append((ty * 4 + tx, {"y": ty, "x": tx}))
    chan_peers = []
    for dz, dc in PEERS[1:]:
        tz, tc = lax.rem(z + dz, 4), lax.rem(core + dc, 2)
        chan_peers.append((tz * 2 + tc, {"z": tz, "core": tc}))
    neighbours = [where for _, where in dp_peers[:4] + chan_peers[:3]]

    def greet(sem):
        for where in neighbours:
            pl.semaphore_signal(sem, 1, device_id=where, device_id_type=MESH_ID)

    greet(barrier)
    loads = []
    for part, source in enumerate((signal, signal_grad)):
        loads.append(pltpu.make_async_copy(source, natural.at[part], input_sem.at[part]))
        loads[-1].start()
    fetches = []
    for at, source in enumerate(stored):
        fetches.append(pltpu.make_async_copy(source, refs[16 + at], table_sem.at[at]))
        fetches[-1].start()
    spectrum[...] = jnp.zeros_like(spectrum)

    for part in range(2):
        loads[part].wait()
        if part == 1:
            pl.semaphore_wait(barrier, 7)
            greet(entered.at[0])

        @pl.loop(0, 4)
        def _(block):
            for tile in range(64):
                piece_of = natural[
                    part, pl.ds(pl.multiple_of(block * 16, 16), 16), 128 * tile : 128 * tile + 128
                ]
                spread[pl.ds(tile, 16, stride=72), :] = piece_of.astype(jnp.float32)
            for peer in range(4):
                for channel in range(4):
                    at = 72 * (4 * peer + channel)
                    both[4 * block + peer, channel, part] = spread[at : at + 64, :].astype(
                        jnp.bfloat16
                    )

    own = pltpu.make_async_copy(both.at[me], arrived.at[0], local_sem)
    own.start()

    def exchange(peers, send, recvs, source, target, nearest=False):
        order = peers if nearest else list(enumerate(peers))
        for at, (index, where) in order if nearest else order[::-1]:
            pltpu.make_async_remote_copy(
                source(index),
                target(at),
                send,
                recvs.at[at] if nearest else recvs,
                device_id=where,
                device_id_type=MESH_ID,
            ).start()

    def all_bytes(buffer, sem, count):
        part = buffer.at[pl.ds(0, count)]
        pltpu.make_async_copy(part, part, sem).wait()

    def over_dp(stage, source, target):
        exchange(dp_peers, dp_send.at[stage], dp_recv.at[stage], source, target)

    def over_chan(stage, source, target):
        exchange(chan_peers, chan_send.at[stage], chan_recv.at[stage], source, target)

    def send_inputs(first_peer, last_peer):
        exchange(
            list(enumerate(dp_peers))[first_peer:last_peer],
            dp_send.at[0],
            arrive_sem,
            lambda index: both.at[index],
            lambda at: arrived.at[at + 1],
            nearest=True,
        )

    send_inputs(0, 4)
    for fetch in fetches:
        fetch.wait()

    table[...] = jnp.zeros_like(table)
    embed_pad[...] = jnp.zeros_like(embed_pad)
    embed_pad[:33, :] = embed_weight[...]
    embed_pad[33:34, :] = embed_bias[...]
    table[33:34, :] = jnp.ones((1, 1024), jnp.float32)
    position = me * 1024 + lax.broadcasted_iota(jnp.int32, (16, 1024), 1)
    lag = jnp.where(me < 8, position, position - 16384)
    phase = ((lag * jnp.concatenate([bands[...]] * 8, axis=1)) & 16383).astype(jnp.float32)
    sines, cosines = sine_cosine(phase * (2.0 * math.pi / 16384))
    table[0:1, :] = lag[:1].astype(jnp.float32) * (1.0 / 8192)
    table[1:17, :] = sines
    table[17:33, :] = cosines
    pl.semaphore_wait(entered.at[0], 7)
    greet(entered.at[1])
    send_inputs(4, 10)
    wide = lambda columns: jnp.concatenate([columns] * 8, axis=1)
    freq_rows = jnp.concatenate([frequency[...]] * 2, axis=1)
    freq_first, freq_second = as_columns(freq_rows[0:1])[:64], as_columns(freq_rows[1:2])[:64]
    sine, cosine = sine_cosine(
        wide(freq_first) * exact_dot(embed_pad[...], table[...], ((0,), (0,)))
    )
    table_kept[...] = kept(table[...])
    sine_first[...] = kept(sine)
    cosine_first[...] = cosine
    pl.semaphore_wait(entered.at[1], 7)
    greet(entered.at[2])
    send_inputs(10, 14)
    sine, cosine = sine_cosine(wide(freq_second) * exact_dot(hidden_weight[...], sine))
    sine_second[...] = kept(sine)
    cosine_second[...] = cosine
    used[0:64, :] = embed_pad[...]
    used[64:128, :] = hidden_weight[...].T
    used[128:130, :] = frequency[...]
    hidden_kept[...] = kept((hidden_weight[...] * freq_second[:, :64]).T)
    decay_columns[...] = as_columns(decay_rate[...])
    output_rows[...] = output_weight[...].T
    weights = output_rows[pl.ds(pl.multiple_of(group * 64, 64), 64), :]
    decay = decay_columns[pl.ds(pl.multiple_of(group * 64, 64), 64), :]
    weights_kept[...] = kept(weights.T)
    distance = jnp.abs(lag[:1]).astype(jnp.float32) * (1.0 / 8192)
    shape = jnp.exp(-wide(decay) * distance) * (1.0 / 128)
    window[...] = shape
    slope[...] = exact_dot(weights, sine) * shape * -distance

    cos_t, sin_t = twist[0], twist[1]

    def add_sequence(slot):
        parts = []
        for part in range(2):
            for channel in range(4):
                data = arrived[slot, channel, part]
                data = jnp.concatenate([data, data], axis=0)
                step = dot(first[...], data)
                real, imag = step[:64], step[64:]
                parts.append(
                    jnp.concatenate(
                        [real * cos_t - imag * sin_t, real * sin_t + imag * cos_t], axis=1
                    )
                )
        high, low = split_values(jnp.concatenate(parts, axis=0))
        whole = dot(jnp.concatenate([high, low, high], axis=1), forward[...])
        in_real, in_imag = whole[:256, :128], whole[:256, 128:]
        grad_real, grad_imag = whole[256:, :128], whole[256:, 128:]
        spectrum[:, :128] += in_real * grad_real + in_imag * grad_imag
        spectrum[:, 128:] += in_real * grad_imag - in_imag * grad_real

    pl.semaphore_wait(entered.at[2], 7)
    send_inputs(14, 15)
    own.wait()
    add_sequence(0)

    @pl.loop(0, 15)
    def _(at):
        pltpu.make_async_remote_copy(
            both.at[0],
            arrived.at[at + 1],
            dp_send.at[0],
            arrive_sem.at[at],
            device_id={"y": y, "x": lax.rem(x + 1, 4)},
            device_id_type=MESH_ID,
        ).wait_recv()
        add_sequence(at + 1)

    high, low = split_values(spectrum[...])
    back = dot(jnp.concatenate([high, low, high], axis=1), backward[...])
    columns = []
    for channel in range(4):
        real = back[64 * channel : 64 * channel + 64, :128]
        imag = back[64 * channel : 64 * channel + 64, 128:]
        columns.append(
            jnp.concatenate([real * cos_t + imag * sin_t, imag * cos_t - real * sin_t], axis=0)
        )
    high, low = split_values(jnp.concatenate(columns, axis=1))
    result = dot(last[...], jnp.concatenate([high, low, high], axis=0))
    lags[...] = result.reshape(16, 8, 512)

    over_dp(1, lambda index: lags.at[index], lambda at: mine.at[me])
    mine[me] = lags[me]
    all_bytes(both, dp_send.at[0], 15)
    all_bytes(mine, dp_recv.at[1], 15)
    for lag_row in range(8):
        for channel in range(4):
            rows[lag_row, pl.ds(channel, 16, stride=4), :] = mine[
                :, lag_row, 128 * channel : 128 * channel + 128
            ]
    over_chan(0, lambda index: rows.at[index], lambda at: landed.at[group])
    landed[group] = rows[group]

    grad = jnp.concatenate([rows[lag_row] for lag_row in range(8)], axis=1)
    high, low = split_values(grad * window[...])
    turned = dot(weights_kept[...], met(high, low, 0)) * cosine_second[...]
    high_second, low_second = split_values(turned)
    turned = dot(hidden_kept[...], met(high_second, low_second, 0)) * cosine_first[...]
    output_grad = lane_dot(met(high, low, 1), sine_second[...])
    hidden_grad = lane_dot(sine_first[...], met(high_second, low_second, 1))
    high, low = split_values(grad * slope[...])
    ones = jnp.ones((8, 2048), jnp.bfloat16)
    decay_row = lane_dot(ones, jnp.concatenate([high, low], axis=1))
    high, low = split_values(turned)
    embed_grad = lane_dot(table_kept[...], met(high, low, 1))

    shared = jnp.concatenate([hidden_grad, embed_grad], axis=1)
    for k in range(4):
        partial[:, k, :] = shared[16 * k : 16 * k + 16]
    packed = jnp.concatenate([output_grad[:32], output_grad[32:]], axis=1)
    for k in range(2):
        partial[:, 4 + k, :] = packed[16 * k : 16 * k + 16]
    decays = jnp.concatenate([decay_row[:1], jnp.zeros((1, 64), jnp.float32)], axis=1)
    partial[:, 6, :] = jnp.broadcast_to(decays, (16, 128))
    partial[:, 7, :] = jnp.zeros((16, 128), jnp.float32)
    over_dp(2, lambda index: partial.at[index], lambda at: partials.at[me])
    partials[me] = partial[me]
    all_bytes(lags, dp_send.at[1], 15)
    all_bytes(rows, chan_send.at[0], 7)
    all_bytes(partials, dp_recv.at[2], 15)
    own_sum[...] = jnp.sum(partials[...], axis=0)
    over_chan(1, lambda index: own_sum, lambda at: group_sums.at[group])
    group_sums[group] = own_sum[...]
    all_bytes(group_sums, chan_recv.at[1], 7)
    summed = jnp.sum(group_sums[...], axis=0)
    piece[0:4, :] = summed[0:4]
    piece[20:24, :] = jnp.zeros((4, 128), jnp.float32)
    for g in range(8):
        piece[4 + 2 * g : 6 + 2 * g, :] = group_sums[g, 4:6, :]
    over_dp(3, lambda index: piece, lambda at: pieces.at[me])
    pieces[me] = piece[...]
    all_bytes(landed, chan_recv.at[0], 7)
    all_bytes(pieces, dp_recv.at[3], 15)
    all_bytes(partial, dp_send.at[2], 15)
    all_bytes(group_sums, chan_send.at[1], 7)
    all_bytes(pieces, dp_send.at[3], 15)


def finish(
    landed,
    pieces,
    group_sums,
    used,
    filter_out,
    embed_out,
    bias_out,
    hidden_out,
    frequency_out,
    output_out,
    decay_out,
    embed,
    bias,
    hidden,
    frequency,
    output_rows,
    output,
    decay,
    sems,
):
    copies = [pltpu.make_async_copy(landed, filter_out, sems.at[0])]
    copies[0].start()

    def send(source, target):
        copies.append(pltpu.make_async_copy(source, target, sems.at[len(copies)]))
        copies[-1].start()

    for g in range(8):
        for k in range(2):
            block = pieces[:, 4 + 2 * g + k, :]
            at = 64 * g + 16 * k
            output_rows[at : at + 16, :] = block[:, :64]
            output_rows[at + 32 : at + 48, :] = block[:, 64:]
    output[...] = output_rows[...].T
    send(output, output_out)
    shared = jnp.concatenate([pieces[:, k, :] for k in range(4)], axis=0)
    scales = jnp.concatenate([used[129:130, :], used[128:129, :]], axis=1)
    scaled = shared * scales
    embed[...] = scaled[:33, 64:]
    send(embed, embed_out)
    bias[...] = scaled[33:34, 64:]
    send(bias, bias_out)
    hidden[...] = scaled.T[:64]
    send(hidden, hidden_out)
    frequency[0:1, :] = jnp.sum(shared[:, 64:] * used[0:64, :], axis=0, keepdims=True)
    frequency[1:2, :] = jnp.sum(shared[:, :64] * used[64:128, :], axis=0, keepdims=True)
    send(frequency, frequency_out)
    for g in range(8):
        decay[0:1, 64 * g : 64 * g + 64] = group_sums[g, 6:7, :64]
    send(decay, decay_out)
    for copy in copies:
        copy.wait()


def local(
    signal,
    signal_grad,
    embed_weight,
    embed_bias,
    hidden_weight,
    frequency,
    output_weight,
    decay_rate,
):
    total = 2 * signal.shape[2]
    scale = 1.0 / math.sqrt(16 * signal.shape[2])
    factors = [max(1, int(0.45 * total * 10000.0 ** (-band / 16))) for band in range(16)]
    bands = np.repeat(np.array(factors, np.int32)[:, None], 128, axis=1)
    tables = transform_tables(total, scale)
    vmem = pl.BlockSpec(memory_space=pltpu.VMEM)
    f32 = jnp.float32
    lags = pltpu.VMEM((64, 1024), f32)
    halves = pltpu.VMEM((64, 3072), jnp.bfloat16)
    stored = [jnp.asarray(t) for t in tables] + [
        jnp.asarray(bands),
        embed_weight.T,
        embed_bias.reshape(1, 64),
        hidden_weight,
        frequency,
        output_weight.T,
        decay_rate.reshape(1, 512),
    ]
    hbm = pl.BlockSpec(memory_space=pltpu.HBM)
    landed, pieces, group_sums, used = pl.pallas_call(
        kernel,
        out_shape=[
            jax.ShapeDtypeStruct(shape, f32) for shape in [(8, 64, 128), (16, 24, 128), (8, 8, 128), (136, 64)]
        ],
        in_specs=[hbm] * 14,
        out_specs=[vmem] * 4,
        scratch_shapes=[
            *[pltpu.VMEM(t.shape, t.dtype) for t in stored],
            pltpu.VMEM((2, 64, 8192), jnp.bfloat16),
            pltpu.VMEM((1152, 128), f32),
            pltpu.VMEM((16, 4, 2, 64, 128), jnp.bfloat16),
            pltpu.VMEM((16, 4, 2, 64, 128), jnp.bfloat16),
            pltpu.VMEM((256, 256), f32),
            pltpu.VMEM((16, 8, 512), f32),
            pltpu.VMEM((16, 8, 512), f32),
            pltpu.VMEM((8, 64, 128), f32),
            lags,
            halves,
            pltpu.VMEM((64, 192), jnp.bfloat16),
            pltpu.VMEM((64, 192), jnp.bfloat16),
            pltpu.VMEM((64, 64), f32),
            pltpu.VMEM((512, 128), f32),
            pltpu.VMEM((512, 64), f32),
            halves,
            lags,
            halves,
            *[lags] * 3,
            pltpu.VMEM((16, 8, 128), f32),
            pltpu.VMEM((16, 8, 128), f32),
            pltpu.VMEM((8, 128), f32),
            pltpu.VMEM((24, 128), f32),
            pltpu.SemaphoreType.DMA,
            pltpu.SemaphoreType.DMA((2,)),
            pltpu.SemaphoreType.DMA((12,)),
            pltpu.SemaphoreType.REGULAR((3,)),
            pltpu.SemaphoreType.DMA((15,)),
            pltpu.SemaphoreType.DMA((4,)),
            pltpu.SemaphoreType.DMA((4,)),
            pltpu.SemaphoreType.DMA((2,)),
            pltpu.SemaphoreType.DMA((2,)),
        ],
        compiler_params=pltpu.CompilerParams(
            collective_id=0, has_side_effects=True, vmem_limit_bytes=40 * 1024 * 1024
        ),
    )(*[pltpu.with_memory_space_constraint(t, pltpu.HBM) for t in (signal[0], signal_grad[0], *stored)])
    shapes = [(512, 128), (33, 64), (1, 64), (64, 64), (2, 64), (64, 512), (1, 512)]
    outs = pl.pallas_call(
        finish,
        out_shape=[jax.ShapeDtypeStruct(shape, f32) for shape in shapes],
        in_specs=[vmem] * 4,
        out_specs=[hbm] * 7,
        scratch_shapes=[
            *[pltpu.VMEM(shape, f32) for shape in shapes[1:5]],
            pltpu.VMEM((512, 64), f32),
            *[pltpu.VMEM(shape, f32) for shape in shapes[5:]],
            pltpu.SemaphoreType.DMA((7,)),
        ],
        compiler_params=pltpu.CompilerParams(vmem_limit_bytes=8 * 1024 * 1024),
    )(landed.reshape(512, 128), pieces, group_sums, used)
    lag_grad, embed_grad, bias_grad, hidden_grad, frequency_grad, output_grad, decay_grad = outs
    return (
        lag_grad,
        embed_grad.T,
        bias_grad.reshape(64),
        hidden_grad,
        frequency_grad,
        output_grad.T,
        decay_grad.reshape(512),
    )


def solution(mesh):
    torus = Mesh(mesh.devices.reshape(4, 4, 4, 2), ("y", "x", "z", "core"))
    return jax.shard_map(
        local,
        mesh=torus,
        in_specs=(P(DP, CHAN, None), P(DP, CHAN, None), P(), P(), P(), P(), P(), P()),
        out_specs=(P(None, DP + CHAN), P(), P(), P(), P(), P(), P()),
        check_vma=False,
    )
```

```python
import math

import jax
import jax.numpy as jnp
import numpy as np
from jax import lax
from jax.experimental import pallas as pl
from jax.experimental.pallas import tpu as pltpu
from jax.sharding import Mesh
from jax.sharding import PartitionSpec as P

DP = ("y", "x")
CHAN = ("z", "core")
MESH_ID = pl.DeviceIdType.MESH
OFFSETS = sorted(
    [(dy, dx) for dy in range(4) for dx in range(4)],
    key=lambda p: (min(p[0], 4 - p[0]) + min(p[1], 4 - p[1])),
)
PEERS = sorted(
    [(dz, dc) for dz in range(4) for dc in range(2)], key=lambda p: (min(p[0], 4 - p[0]) + p[1])
)


def split_table(values):
    high = values.astype(jnp.bfloat16)
    low = (values - high.astype(np.float64)).astype(jnp.bfloat16)
    return high, low


def transform_tables(total, scale):
    half, side = 64, 128
    k1 = np.arange(half)[:, None] + 0.5
    n1 = np.arange(half)[None, :]
    angle = -2.0 * np.pi * k1 * n1 / side
    first = np.concatenate([np.cos(angle), np.sin(angle)], axis=0)
    first = np.concatenate(split_table(first), axis=1)
    n2 = np.arange(side)[None, :]
    angle = -2.0 * np.pi * k1 * n2 / total
    twist = np.stack([np.cos(angle), np.sin(angle)]).astype(np.float32)
    rows = np.arange(side)[:, None]
    angle = -2.0 * np.pi * (rows * n2 % side) / side
    cosine, sine = np.cos(angle), np.sin(angle)
    forward = np.block([[cosine, sine], [-sine, cosine]])
    high, low = split_table(forward)
    forward = np.concatenate([high, high, low], axis=0)
    backward = np.block([[cosine, -sine], [sine, cosine]])
    high, low = split_table(backward)
    backward = np.concatenate([high, high, low], axis=0)
    lag_row = np.arange(side)[:, None]
    freq = np.arange(half)[None, :] + 0.5
    angle = 2.0 * np.pi * lag_row * freq / side
    last = np.concatenate([np.cos(angle), -np.sin(angle)], axis=1)
    last = last * np.where(lag_row < half, 1.0, -1.0) * (2.0 * scale / total)
    high, low = split_table(last)
    last = np.concatenate([high, high, low], axis=1)
    return first, twist, forward, backward, last


def split_values(values):
    high = values.astype(jnp.bfloat16)
    low = (values - high.astype(jnp.float32)).astype(jnp.bfloat16)
    return high, low


def dot(a, b):
    return jnp.dot(a, b, preferred_element_type=jnp.float32)


def lane_dot(a, b):
    return lax.dot_general(a, b, (((1,), (1,)), ((), ())), preferred_element_type=jnp.float32)


def kept(values):
    high, low = split_values(values)
    return jnp.concatenate([high, high, low], axis=1)


def met(high, low, axis):
    return jnp.concatenate([high, low, high], axis=axis)


def exact_dot(a, b, dims=((1,), (0,))):
    return lax.dot_general(
        a, b, (dims, ((), ())), precision=lax.Precision.HIGHEST, preferred_element_type=jnp.float32
    )


def sine_cosine(angle):
    turns = jnp.floor(angle * (2.0 / math.pi) + 0.5)
    rest = angle - turns * 1.5703125
    rest = rest - turns * 4.837512969970703125e-4
    rest = rest - turns * 7.54978995489188216e-8
    square = rest * rest
    sine = -1.9515295891e-4 * square + 8.3321608736e-3
    sine = sine * square - 1.6666654611e-1
    sine = sine * square * rest + rest
    cosine = 2.443315711809948e-5 * square - 1.388731625493765e-3
    cosine = cosine * square + 4.166664568298827e-2
    cosine = cosine * square * square - 0.5 * square + 1.0
    quarter = turns.astype(jnp.int32)
    odd = (quarter & 1) == 1
    first = jnp.where(odd, cosine, sine)
    second = jnp.where(odd, sine, cosine)
    first = jnp.where((quarter & 2) == 2, -first, first)
    second = jnp.where(((quarter + 1) & 2) == 2, -second, second)
    return first, second


def as_columns(row):
    return jnp.broadcast_to(row, (128, row.shape[1])).T


def kernel(
    signal,
    signal_grad,
    *refs,
):
    (
        *stored,
        landed,
        pieces,
        group_sums,
        used,
        first,
        twist,
        forward,
        backward,
        last,
        bands,
        embed_weight,
        embed_bias,
        hidden_weight,
        frequency,
        output_weight,
        decay_rate,
        natural,
        spread,
        both,
        arrived,
        spectrum,
        lags,
        mine,
        rows,
        table,
        table_kept,
        weights_kept,
        hidden_kept,
        embed_pad,
        decay_columns,
        output_rows,
        sine_first,
        cosine_first,
        sine_second,
        cosine_second,
        window,
        slope,
        partial,
        partials,
        own_sum,
        piece,
        local_sem,
        input_sem,
        table_sem,
        entered,
        arrive_sem,
        dp_send,
        dp_recv,
        chan_send,
        chan_recv,
    ) = refs
    y, x = lax.axis_index("y"), lax.axis_index("x")
    z, core = lax.axis_index("z"), lax.axis_index("core")
    me = y * 4 + x
    group = z * 2 + core

    barrier = pltpu.get_barrier_semaphore()
    dp_peers = []
    for dy, dx in OFFSETS[1:]:
        ty, tx = lax.rem(y + dy, 4), lax.rem(x + dx, 4)
        dp_peers.append((ty * 4 + tx, {"y": ty, "x": tx}))
    chan_peers = []
    for dz, dc in PEERS[1:]:
        tz, tc = lax.rem(z + dz, 4), lax.rem(core + dc, 2)
        chan_peers.append((tz * 2 + tc, {"z": tz, "core": tc}))
    neighbours = [where for _, where in dp_peers[:4] + chan_peers[:3]]

    def greet(sem):
        for where in neighbours:
            pl.semaphore_signal(sem, 1, device_id=where, device_id_type=MESH_ID)

    greet(barrier)
    blocks = [lax.rem(y + step, 4) for step in (0, 1, 3, 2)]
    loads = []
    for at, block in enumerate(blocks):
        some = pl.ds(pl.multiple_of(block * 16, 16), 16)
        for part, source in enumerate((signal, signal_grad)):
            loads.append(
                pltpu.make_async_copy(
                    source.at[some], natural.at[part, at], input_sem.at[2 * at + part]
                )
            )
            loads[-1].start()
    fetches = []
    for at, source in enumerate(stored):
        fetches.append(pltpu.make_async_copy(source, refs[16 + at], table_sem.at[at]))
        fetches[-1].start()
    spectrum[...] = jnp.zeros_like(spectrum)
    partial[:, 7, :] = jnp.zeros((16, 128), jnp.float32)

    def exchange(peers, send, recvs, source, target, nearest=False):
        order = peers if nearest else list(enumerate(peers))
        for at, (index, where) in order if nearest else order[::-1]:
            pltpu.make_async_remote_copy(
                source(index),
                target(at),
                send,
                recvs.at[at] if nearest else recvs,
                device_id=where,
                device_id_type=MESH_ID,
            ).start()

    def all_bytes(buffer, sem, count):
        part = buffer.at[pl.ds(0, count)]
        pltpu.make_async_copy(part, part, sem).wait()

    def over_dp(stage, source, target):
        exchange(dp_peers, dp_send.at[stage], dp_recv.at[stage], source, target)

    def over_chan(stage, source, target):
        exchange(chan_peers, chan_send.at[stage], chan_recv.at[stage], source, target)

    def send_inputs(*offsets):
        ranks = [OFFSETS.index(offset) - 1 for offset in offsets]
        exchange(
            [(rank, dp_peers[rank]) for rank in ranks],
            dp_send.at[0],
            arrive_sem,
            lambda index: both.at[index],
            lambda at: arrived.at[at + 1],
            nearest=True,
        )

    def lay_out(at):
        for part in range(2):
            loads[2 * at + part].wait()
            for tile in range(64):
                some = natural[part, at, :, 128 * tile : 128 * tile + 128]
                spread[part, pl.ds(tile, 16, stride=72), :] = some.astype(jnp.float32)
            for peer in range(4):
                for channel in range(4):
                    row = 72 * (4 * peer + channel)
                    both[4 * blocks[at] + peer, channel, part] = spread[
                        part, row : row + 64, :
                    ].astype(jnp.bfloat16)

    lay_out(0)
    pl.semaphore_wait(barrier, 7)
    greet(entered.at[0])
    send_inputs((0, 1), (0, 3))
    lay_out(1)
    send_inputs((1, 0))
    lay_out(2)
    send_inputs((3, 0))
    pl.semaphore_wait(entered.at[0], 7)
    greet(entered.at[1])
    lay_out(3)
    own = pltpu.make_async_copy(both.at[me], arrived.at[0], local_sem)
    own.start()
    send_inputs((0, 2), (1, 1), (1, 3), (2, 0), (3, 1), (3, 3))

    for fetch in fetches:
        fetch.wait()

    table[...] = jnp.zeros_like(table)
    embed_pad[...] = jnp.zeros_like(embed_pad)
    embed_pad[:33, :] = embed_weight[...]
    embed_pad[33:34, :] = embed_bias[...]
    table[33:34, :] = jnp.ones((1, 1024), jnp.float32)
    position = me * 1024 + lax.broadcasted_iota(jnp.int32, (16, 1024), 1)
    lag = jnp.where(me < 8, position, position - 16384)
    phase = ((lag * jnp.concatenate([bands[...]] * 8, axis=1)) & 16383).astype(jnp.float32)
    sines, cosines = sine_cosine(phase * (2.0 * math.pi / 16384))
    table[0:1, :] = lag[:1].astype(jnp.float32) * (1.0 / 8192)
    table[1:17, :] = sines
    table[17:33, :] = cosines
    wide = lambda columns: jnp.concatenate([columns] * 8, axis=1)
    freq_rows = jnp.concatenate([frequency[...]] * 2, axis=1)
    freq_first, freq_second = as_columns(freq_rows[0:1])[:64], as_columns(freq_rows[1:2])[:64]
    sine, cosine = sine_cosine(
        wide(freq_first) * exact_dot(embed_pad[...], table[...], ((0,), (0,)))
    )
    table_kept[...] = kept(table[...])
    sine_first[...] = kept(sine)
    cosine_first[...] = cosine
    pl.semaphore_wait(entered.at[1], 7)
    greet(entered.at[2])
    send_inputs((1, 2), (2, 1), (2, 3), (3, 2))
    sine, cosine = sine_cosine(wide(freq_second) * exact_dot(hidden_weight[...], sine))
    sine_second[...] = kept(sine)
    cosine_second[...] = cosine
    used[0:64, :] = embed_pad[...]
    used[64:128, :] = hidden_weight[...].T
    used[128:130, :] = frequency[...]
    hidden_kept[...] = kept((hidden_weight[...] * freq_second[:, :64]).T)
    decay_columns[...] = as_columns(decay_rate[...])
    output_rows[...] = output_weight[...].T
    weights = output_rows[pl.ds(pl.multiple_of(group * 64, 64), 64), :]
    decay = decay_columns[pl.ds(pl.multiple_of(group * 64, 64), 64), :]
    weights_kept[...] = kept(weights.T)
    distance = jnp.abs(lag[:1]).astype(jnp.float32) * (1.0 / 8192)
    shape = jnp.exp(-wide(decay) * distance) * (1.0 / 128)
    window[...] = shape
    slope[...] = exact_dot(weights, sine) * shape * -distance

    cos_t, sin_t = twist[0], twist[1]

    def add_sequence(slot):
        parts = []
        for part in range(2):
            for channel in range(4):
                data = arrived[slot, channel, part]
                data = jnp.concatenate([data, data], axis=0)
                step = dot(first[...], data)
                real, imag = step[:64], step[64:]
                parts.append(
                    jnp.concatenate(
                        [real * cos_t - imag * sin_t, real * sin_t + imag * cos_t], axis=1
                    )
                )
        high, low = split_values(jnp.concatenate(parts, axis=0))
        whole = dot(jnp.concatenate([high, low, high], axis=1), forward[...])
        in_real, in_imag = whole[:256, :128], whole[:256, 128:]
        grad_real, grad_imag = whole[256:, :128], whole[256:, 128:]
        spectrum[:, :128] += in_real * grad_real + in_imag * grad_imag
        spectrum[:, 128:] += in_real * grad_imag - in_imag * grad_real

    pl.semaphore_wait(entered.at[2], 7)
    send_inputs((2, 2))
    own.wait()
    add_sequence(0)

    @pl.loop(0, 15)
    def _(at):
        pltpu.make_async_remote_copy(
            both.at[0],
            arrived.at[at + 1],
            dp_send.at[0],
            arrive_sem.at[at],
            device_id={"y": y, "x": lax.rem(x + 1, 4)},
            device_id_type=MESH_ID,
        ).wait_recv()
        add_sequence(at + 1)

    high, low = split_values(spectrum[...])
    back = dot(jnp.concatenate([high, low, high], axis=1), backward[...])
    columns = []
    for channel in range(4):
        real = back[64 * channel : 64 * channel + 64, :128]
        imag = back[64 * channel : 64 * channel + 64, 128:]
        columns.append(
            jnp.concatenate([real * cos_t + imag * sin_t, imag * cos_t - real * sin_t], axis=0)
        )
    high, low = split_values(jnp.concatenate(columns, axis=1))
    result = dot(last[...], jnp.concatenate([high, low, high], axis=0))
    lags[...] = result.reshape(16, 8, 512)

    over_dp(1, lambda index: lags.at[index], lambda at: mine.at[me])
    mine[me] = lags[me]
    all_bytes(both, dp_send.at[0], 15)
    all_bytes(mine, dp_recv.at[1], 15)
    for lag_row in range(8):
        for channel in range(4):
            rows[lag_row, pl.ds(channel, 16, stride=4), :] = mine[
                :, lag_row, 128 * channel : 128 * channel + 128
            ]

    grad = jnp.concatenate([rows[lag_row] for lag_row in range(8)], axis=1)
    high, low = split_values(grad * window[...])
    turned = dot(weights_kept[...], met(high, low, 0)) * cosine_second[...]
    high_second, low_second = split_values(turned)
    turned = dot(hidden_kept[...], met(high_second, low_second, 0)) * cosine_first[...]
    output_grad = lane_dot(met(high, low, 1), sine_second[...])
    hidden_grad = lane_dot(sine_first[...], met(high_second, low_second, 1))
    high, low = split_values(grad * slope[...])
    ones = jnp.ones((8, 2048), jnp.bfloat16)
    decay_row = lane_dot(ones, jnp.concatenate([high, low], axis=1))
    high, low = split_values(turned)
    embed_grad = lane_dot(table_kept[...], met(high, low, 1))

    shared = jnp.concatenate([hidden_grad, embed_grad], axis=1)
    for k in range(4):
        partial[:, k, :] = shared[16 * k : 16 * k + 16]
    packed = jnp.concatenate([output_grad[:32], output_grad[32:]], axis=1)
    for k in range(2):
        partial[:, 4 + k, :] = packed[16 * k : 16 * k + 16]
    decays = jnp.concatenate([decay_row[:1], jnp.zeros((1, 64), jnp.float32)], axis=1)
    partial[:, 6, :] = jnp.broadcast_to(decays, (16, 128))
    over_dp(2, lambda index: partial.at[index], lambda at: partials.at[me])
    partials[me] = partial[me]
    over_chan(0, lambda index: rows.at[index], lambda at: landed.at[group])
    landed[group] = rows[group]
    all_bytes(lags, dp_send.at[1], 15)
    all_bytes(rows, chan_send.at[0], 7)
    all_bytes(partials, dp_recv.at[2], 15)
    own_sum[...] = jnp.sum(partials[...], axis=0)
    over_chan(1, lambda index: own_sum, lambda at: group_sums.at[group])
    group_sums[group] = own_sum[...]
    all_bytes(group_sums, chan_recv.at[1], 7)
    summed = jnp.sum(group_sums[...], axis=0)
    piece[0:4, :] = summed[0:4]
    for g in range(8):
        piece[4 + 2 * g : 6 + 2 * g, :] = group_sums[g, 4:6, :]
    over_dp(3, lambda index: piece, lambda at: pieces.at[me])
    pieces[me] = piece[...]
    all_bytes(landed, chan_recv.at[0], 7)
    all_bytes(pieces, dp_recv.at[3], 15)
    all_bytes(partial, dp_send.at[2], 15)
    all_bytes(group_sums, chan_send.at[1], 7)
    all_bytes(pieces, dp_send.at[3], 15)


def finish(
    landed,
    pieces,
    group_sums,
    used,
    filter_out,
    embed_out,
    bias_out,
    hidden_out,
    frequency_out,
    output_out,
    decay_out,
    embed,
    bias,
    hidden,
    frequency,
    output_rows,
    output,
    decay,
    sems,
):
    copies = [pltpu.make_async_copy(landed, filter_out, sems.at[0])]
    copies[0].start()

    def send(source, target):
        copies.append(pltpu.make_async_copy(source, target, sems.at[len(copies)]))
        copies[-1].start()

    for g in range(8):
        for k in range(2):
            block = pieces[:, 4 + 2 * g + k, :]
            at = 64 * g + 16 * k
            output_rows[at : at + 16, :] = block[:, :64]
            output_rows[at + 32 : at + 48, :] = block[:, 64:]
    output[...] = output_rows[...].T
    send(output, output_out)
    shared = jnp.concatenate([pieces[:, k, :] for k in range(4)], axis=0)
    scales = jnp.concatenate([used[129:130, :], used[128:129, :]], axis=1)
    scaled = shared * scales
    embed[...] = scaled[:33, 64:]
    send(embed, embed_out)
    bias[...] = scaled[33:34, 64:]
    send(bias, bias_out)
    hidden[...] = scaled.T[:64]
    send(hidden, hidden_out)
    frequency[0:1, :] = jnp.sum(shared[:, 64:] * used[0:64, :], axis=0, keepdims=True)
    frequency[1:2, :] = jnp.sum(shared[:, :64] * used[64:128, :], axis=0, keepdims=True)
    send(frequency, frequency_out)
    for g in range(8):
        decay[0:1, 64 * g : 64 * g + 64] = group_sums[g, 6:7, :64]
    send(decay, decay_out)
    for copy in copies:
        copy.wait()


def local(
    signal,
    signal_grad,
    embed_weight,
    embed_bias,
    hidden_weight,
    frequency,
    output_weight,
    decay_rate,
):
    total = 2 * signal.shape[2]
    scale = 1.0 / math.sqrt(16 * signal.shape[2])
    factors = [max(1, int(0.45 * total * 10000.0 ** (-band / 16))) for band in range(16)]
    bands = np.repeat(np.array(factors, np.int32)[:, None], 128, axis=1)
    tables = transform_tables(total, scale)
    vmem = pl.BlockSpec(memory_space=pltpu.VMEM)
    f32 = jnp.float32
    lags = pltpu.VMEM((64, 1024), f32)
    halves = pltpu.VMEM((64, 3072), jnp.bfloat16)
    stored = [jnp.asarray(t) for t in tables] + [
        jnp.asarray(bands),
        embed_weight.T,
        embed_bias.reshape(1, 64),
        hidden_weight,
        frequency,
        output_weight.T,
        decay_rate.reshape(1, 512),
    ]
    hbm = pl.BlockSpec(memory_space=pltpu.HBM)
    landed, pieces, group_sums, used = pl.pallas_call(
        kernel,
        out_shape=[
            jax.ShapeDtypeStruct(shape, f32) for shape in [(8, 64, 128), (16, 20, 128), (8, 8, 128), (136, 64)]
        ],
        in_specs=[hbm] * 14,
        out_specs=[vmem] * 4,
        scratch_shapes=[
            *[pltpu.VMEM(t.shape, t.dtype) for t in stored],
            pltpu.VMEM((2, 4, 16, 8192), jnp.bfloat16),
            pltpu.VMEM((2, 1152, 128), f32),
            pltpu.VMEM((16, 4, 2, 64, 128), jnp.bfloat16),
            pltpu.VMEM((16, 4, 2, 64, 128), jnp.bfloat16),
            pltpu.VMEM((256, 256), f32),
            pltpu.VMEM((16, 8, 512), f32),
            pltpu.VMEM((16, 8, 512), f32),
            pltpu.VMEM((8, 64, 128), f32),
            lags,
            halves,
            pltpu.VMEM((64, 192), jnp.bfloat16),
            pltpu.VMEM((64, 192), jnp.bfloat16),
            pltpu.VMEM((64, 64), f32),
            pltpu.VMEM((512, 128), f32),
            pltpu.VMEM((512, 64), f32),
            halves,
            lags,
            halves,
            *[lags] * 3,
            pltpu.VMEM((16, 8, 128), f32),
            pltpu.VMEM((16, 8, 128), f32),
            pltpu.VMEM((8, 128), f32),
            pltpu.VMEM((20, 128), f32),
            pltpu.SemaphoreType.DMA,
            pltpu.SemaphoreType.DMA((8,)),
            pltpu.SemaphoreType.DMA((12,)),
            pltpu.SemaphoreType.REGULAR((3,)),
            pltpu.SemaphoreType.DMA((15,)),
            pltpu.SemaphoreType.DMA((4,)),
            pltpu.SemaphoreType.DMA((4,)),
            pltpu.SemaphoreType.DMA((2,)),
            pltpu.SemaphoreType.DMA((2,)),
        ],
        compiler_params=pltpu.CompilerParams(
            collective_id=0, has_side_effects=True, vmem_limit_bytes=40 * 1024 * 1024
        ),
    )(*[pltpu.with_memory_space_constraint(t, pltpu.HBM) for t in (signal[0], signal_grad[0], *stored)])
    shapes = [(512, 128), (33, 64), (1, 64), (64, 64), (2, 64), (64, 512), (1, 512)]
    outs = pl.pallas_call(
        finish,
        out_shape=[jax.ShapeDtypeStruct(shape, f32) for shape in shapes],
        in_specs=[vmem] * 4,
        out_specs=[hbm] * 7,
        scratch_shapes=[
            *[pltpu.VMEM(shape, f32) for shape in shapes[1:5]],
            pltpu.VMEM((512, 64), f32),
            *[pltpu.VMEM(shape, f32) for shape in shapes[5:]],
            pltpu.SemaphoreType.DMA((7,)),
        ],
        compiler_params=pltpu.CompilerParams(vmem_limit_bytes=8 * 1024 * 1024),
    )(landed.reshape(512, 128), pieces, group_sums, used)
    lag_grad, embed_grad, bias_grad, hidden_grad, frequency_grad, output_grad, decay_grad = outs
    return (
        lag_grad,
        embed_grad.T,
        bias_grad.reshape(64),
        hidden_grad,
        frequency_grad,
        output_grad.T,
        decay_grad.reshape(512),
    )


def solution(mesh):
    torus = Mesh(mesh.devices.reshape(4, 4, 4, 2), ("y", "x", "z", "core"))
    return jax.shard_map(
        local,
        mesh=torus,
        in_specs=(P(DP, CHAN, None), P(DP, CHAN, None), P(), P(), P(), P(), P(), P()),
        out_specs=(P(None, DP + CHAN), P(), P(), P(), P(), P(), P()),
        check_vma=False,
    )
```

```python
import math

import jax
import jax.numpy as jnp
import numpy as np
from jax import lax
from jax.experimental import pallas as pl
from jax.experimental.pallas import tpu as pltpu
from jax.sharding import Mesh
from jax.sharding import PartitionSpec as P

DP = ("y", "x")
CHAN = ("z", "core")
MESH_ID = pl.DeviceIdType.MESH
OFFSETS = sorted(
    [(dy, dx) for dy in range(4) for dx in range(4)],
    key=lambda p: (min(p[0], 4 - p[0]) + min(p[1], 4 - p[1])),
)
PEERS = sorted(
    [(dz, dc) for dz in range(4) for dc in range(2)], key=lambda p: (min(p[0], 4 - p[0]) + p[1])
)


def split_table(values):
    high = values.astype(jnp.bfloat16)
    low = (values - high.astype(np.float64)).astype(jnp.bfloat16)
    return high, low


def transform_tables(total, scale):
    half, side = 64, 128
    k1 = np.arange(half)[:, None] + 0.5
    n1 = np.arange(half)[None, :]
    angle = -2.0 * np.pi * k1 * n1 / side
    first = np.concatenate([np.cos(angle), np.sin(angle)], axis=0)
    first = np.concatenate(split_table(first), axis=1)
    n2 = np.arange(side)[None, :]
    angle = -2.0 * np.pi * k1 * n2 / total
    twist = np.stack([np.cos(angle), np.sin(angle)]).astype(np.float32)
    rows = np.arange(side)[:, None]
    angle = -2.0 * np.pi * (rows * n2 % side) / side
    cosine, sine = np.cos(angle), np.sin(angle)
    forward = np.block([[cosine, sine], [-sine, cosine]])
    high, low = split_table(forward)
    forward = np.concatenate([high, high, low], axis=0)
    backward = np.block([[cosine, -sine], [sine, cosine]])
    high, low = split_table(backward)
    backward = np.concatenate([high, high, low], axis=0)
    lag_row = np.arange(side)[:, None]
    freq = np.arange(half)[None, :] + 0.5
    angle = 2.0 * np.pi * lag_row * freq / side
    last = np.concatenate([np.cos(angle), -np.sin(angle)], axis=1)
    last = last * np.where(lag_row < half, 1.0, -1.0) * (2.0 * scale / total)
    high, low = split_table(last)
    last = np.concatenate([high, high, low], axis=1)
    return first, twist, forward, backward, last


def split_values(values):
    high = values.astype(jnp.bfloat16)
    low = (values - high.astype(jnp.float32)).astype(jnp.bfloat16)
    return high, low


def dot(a, b):
    return jnp.dot(a, b, preferred_element_type=jnp.float32)


def lane_dot(a, b):
    return lax.dot_general(a, b, (((1,), (1,)), ((), ())), preferred_element_type=jnp.float32)


def kept(values):
    high, low = split_values(values)
    return jnp.concatenate([high, high, low], axis=1)


def met(high, low, axis):
    return jnp.concatenate([high, low, high], axis=axis)


def exact_dot(a, b, dims=((1,), (0,))):
    return lax.dot_general(
        a, b, (dims, ((), ())), precision=lax.Precision.HIGHEST, preferred_element_type=jnp.float32
    )


def sine_cosine(angle):
    turns = jnp.floor(angle * (2.0 / math.pi) + 0.5)
    rest = angle - turns * 1.5703125
    rest = rest - turns * 4.837512969970703125e-4
    rest = rest - turns * 7.54978995489188216e-8
    square = rest * rest
    sine = -1.9515295891e-4 * square + 8.3321608736e-3
    sine = sine * square - 1.6666654611e-1
    sine = sine * square * rest + rest
    cosine = 2.443315711809948e-5 * square - 1.388731625493765e-3
    cosine = cosine * square + 4.166664568298827e-2
    cosine = cosine * square * square - 0.5 * square + 1.0
    quarter = turns.astype(jnp.int32)
    odd = (quarter & 1) == 1
    first = jnp.where(odd, cosine, sine)
    second = jnp.where(odd, sine, cosine)
    first = jnp.where((quarter & 2) == 2, -first, first)
    second = jnp.where(((quarter + 1) & 2) == 2, -second, second)
    return first, second


def as_columns(row):
    return jnp.broadcast_to(row, (128, row.shape[1])).T


def kernel(
    signal,
    signal_grad,
    *refs,
):
    (
        *stored,
        landed,
        pieces,
        group_sums,
        used,
        first,
        twist,
        forward,
        backward,
        last,
        bands,
        embed_weight,
        embed_bias,
        hidden_weight,
        frequency,
        output_weight,
        decay_rate,
        natural,
        spread,
        both,
        arrived,
        spectrum,
        lags,
        mine,
        rows,
        table,
        table_kept,
        weights_kept,
        hidden_kept,
        embed_pad,
        decay_columns,
        output_rows,
        sine_first,
        cosine_first,
        sine_second,
        cosine_second,
        window,
        slope,
        partial,
        partials,
        own_sum,
        piece,
        local_sem,
        input_sem,
        table_sem,
        entered,
        arrive_sem,
        dp_send,
        dp_recv,
        chan_send,
        chan_recv,
    ) = refs
    y, x = lax.axis_index("y"), lax.axis_index("x")
    z, core = lax.axis_index("z"), lax.axis_index("core")
    me = y * 4 + x
    group = z * 2 + core

    barrier = pltpu.get_barrier_semaphore()
    dp_peers = []
    for dy, dx in OFFSETS[1:]:
        ty, tx = lax.rem(y + dy, 4), lax.rem(x + dx, 4)
        dp_peers.append((ty * 4 + tx, {"y": ty, "x": tx}))
    chan_peers = []
    for dz, dc in PEERS[1:]:
        tz, tc = lax.rem(z + dz, 4), lax.rem(core + dc, 2)
        chan_peers.append((tz * 2 + tc, {"z": tz, "core": tc}))
    neighbours = [where for _, where in dp_peers[:4] + chan_peers[:3]]

    def greet(sem):
        for where in neighbours:
            pl.semaphore_signal(sem, 1, device_id=where, device_id_type=MESH_ID)

    greet(barrier)
    blocks = [lax.rem(y + step, 4) for step in (0, 1, 3, 2)]
    loads = []
    for at, block in enumerate(blocks):
        some = pl.ds(pl.multiple_of(block * 16, 16), 16)
        for part, source in enumerate((signal, signal_grad)):
            loads.append(
                pltpu.make_async_copy(
                    source.at[some], natural.at[part, at], input_sem.at[2 * at + part]
                )
            )
            loads[-1].start()
    fetches = []
    for at, source in enumerate(stored):
        fetches.append(pltpu.make_async_copy(source, refs[16 + at], table_sem.at[at]))
        fetches[-1].start()
    spectrum[...] = jnp.zeros_like(spectrum)
    partial[:, 7, :] = jnp.zeros((16, 128), jnp.float32)

    def exchange(peers, send, recvs, source, target, nearest=False):
        order = peers if nearest else list(enumerate(peers))
        for at, (index, where) in order if nearest else order[::-1]:
            pltpu.make_async_remote_copy(
                source(index),
                target(at),
                send,
                recvs.at[at] if nearest else recvs,
                device_id=where,
                device_id_type=MESH_ID,
            ).start()

    def all_bytes(buffer, sem, count):
        part = buffer.at[pl.ds(0, count)]
        pltpu.make_async_copy(part, part, sem).wait()

    def over_dp(stage, source, target):
        exchange(dp_peers, dp_send.at[stage], dp_recv.at[stage], source, target)

    def over_chan(stage, source, target):
        exchange(chan_peers, chan_send.at[stage], chan_recv.at[stage], source, target)

    def send_inputs(*offsets):
        ranks = [OFFSETS.index(offset) - 1 for offset in offsets]
        exchange(
            [(rank, dp_peers[rank]) for rank in ranks],
            dp_send.at[0],
            arrive_sem,
            lambda index: both.at[index],
            lambda at: arrived.at[at + 1],
            nearest=True,
        )

    def lay_out(at):
        for part in range(2):
            loads[2 * at + part].wait()
            for tile in range(64):
                some = natural[part, at, :, 128 * tile : 128 * tile + 128]
                spread[part, pl.ds(tile, 16, stride=72), :] = some.astype(jnp.float32)
            for peer in range(4):
                for channel in range(4):
                    row = 72 * (4 * peer + channel)
                    both[4 * blocks[at] + peer, channel, part] = spread[
                        part, row : row + 64, :
                    ].astype(jnp.bfloat16)

    lay_out(0)
    pl.semaphore_wait(barrier, 7)
    greet(entered.at[0])
    send_inputs((0, 1), (0, 3))
    lay_out(1)
    send_inputs((1, 0))
    lay_out(2)
    send_inputs((3, 0))
    pl.semaphore_wait(entered.at[0], 7)
    greet(entered.at[1])
    lay_out(3)
    own = pltpu.make_async_copy(both.at[me], arrived.at[0], local_sem)
    own.start()
    send_inputs((0, 2), (1, 1), (1, 3), (2, 0), (3, 1), (3, 3))

    for fetch in fetches:
        fetch.wait()

    table[...] = jnp.zeros_like(table)
    embed_pad[...] = jnp.zeros_like(embed_pad)
    embed_pad[:33, :] = embed_weight[...]
    embed_pad[33:34, :] = embed_bias[...]
    table[33:34, :] = jnp.ones((1, 1024), jnp.float32)
    position = me * 1024 + lax.broadcasted_iota(jnp.int32, (16, 1024), 1)
    lag = jnp.where(me < 8, position, position - 16384)
    phase = ((lag * jnp.concatenate([bands[...]] * 8, axis=1)) & 16383).astype(jnp.float32)
    sines, cosines = sine_cosine(phase * (2.0 * math.pi / 16384))
    table[0:1, :] = lag[:1].astype(jnp.float32) * (1.0 / 8192)
    table[1:17, :] = sines
    table[17:33, :] = cosines
    wide = lambda columns: jnp.concatenate([columns] * 8, axis=1)
    freq_rows = jnp.concatenate([frequency[...]] * 2, axis=1)
    freq_first, freq_second = as_columns(freq_rows[0:1])[:64], as_columns(freq_rows[1:2])[:64]
    sine, cosine = sine_cosine(
        wide(freq_first) * exact_dot(embed_pad[...], table[...], ((0,), (0,)))
    )
    table_kept[...] = kept(table[...])
    sine_first[...] = kept(sine)
    cosine_first[...] = cosine
    pl.semaphore_wait(entered.at[1], 7)
    for _, where in dp_peers[:4]:
        pl.semaphore_signal(entered.at[2], 1, device_id=where, device_id_type=MESH_ID)
    send_inputs((1, 2), (2, 1), (2, 3), (3, 2))
    sine, cosine = sine_cosine(wide(freq_second) * exact_dot(hidden_weight[...], sine))
    sine_second[...] = kept(sine)
    cosine_second[...] = cosine
    used[0:64, :] = embed_pad[...]
    used[64:128, :] = hidden_weight[...].T
    used[128:130, :] = frequency[...]
    hidden_kept[...] = kept((hidden_weight[...] * freq_second[:, :64]).T)
    decay_columns[...] = as_columns(decay_rate[...])
    output_rows[...] = output_weight[...].T
    weights = output_rows[pl.ds(pl.multiple_of(group * 64, 64), 64), :]
    decay = decay_columns[pl.ds(pl.multiple_of(group * 64, 64), 64), :]
    weights_kept[...] = kept(weights.T)
    distance = jnp.abs(lag[:1]).astype(jnp.float32) * (1.0 / 8192)
    shape = jnp.exp(-wide(decay) * distance) * (1.0 / 128)
    window[...] = shape
    slope[...] = exact_dot(weights, sine) * shape * -distance

    cos_t, sin_t = twist[0], twist[1]

    def add_sequence(slot):
        parts = []
        for part in range(2):
            for channel in range(4):
                data = arrived[slot, channel, part]
                data = jnp.concatenate([data, data], axis=0)
                step = dot(first[...], data)
                real, imag = step[:64], step[64:]
                parts.append(
                    jnp.concatenate(
                        [real * cos_t - imag * sin_t, real * sin_t + imag * cos_t], axis=1
                    )
                )
        high, low = split_values(jnp.concatenate(parts, axis=0))
        whole = dot(jnp.concatenate([high, low, high], axis=1), forward[...])
        in_real, in_imag = whole[:256, :128], whole[:256, 128:]
        grad_real, grad_imag = whole[256:, :128], whole[256:, 128:]
        spectrum[:, :128] += in_real * grad_real + in_imag * grad_imag
        spectrum[:, 128:] += in_real * grad_imag - in_imag * grad_real

    pl.semaphore_wait(entered.at[2], 4)
    send_inputs((2, 2))
    own.wait()
    add_sequence(0)

    @pl.loop(0, 15)
    def _(at):
        pltpu.make_async_remote_copy(
            both.at[0],
            arrived.at[at + 1],
            dp_send.at[0],
            arrive_sem.at[at],
            device_id={"y": y, "x": lax.rem(x + 1, 4)},
            device_id_type=MESH_ID,
        ).wait_recv()
        add_sequence(at + 1)

    high, low = split_values(spectrum[...])
    back = dot(jnp.concatenate([high, low, high], axis=1), backward[...])
    columns = []
    for channel in range(4):
        real = back[64 * channel : 64 * channel + 64, :128]
        imag = back[64 * channel : 64 * channel + 64, 128:]
        columns.append(
            jnp.concatenate([real * cos_t + imag * sin_t, imag * cos_t - real * sin_t], axis=0)
        )
    high, low = split_values(jnp.concatenate(columns, axis=1))
    result = dot(last[...], jnp.concatenate([high, low, high], axis=0))
    lags[...] = result.reshape(16, 8, 512)

    over_dp(1, lambda index: lags.at[index], lambda at: mine.at[me])
    mine[me] = lags[me]
    all_bytes(both, dp_send.at[0], 15)
    all_bytes(mine, dp_recv.at[1], 15)
    for lag_row in range(8):
        for channel in range(4):
            rows[lag_row, pl.ds(channel, 16, stride=4), :] = mine[
                :, lag_row, 128 * channel : 128 * channel + 128
            ]

    grad = jnp.concatenate([rows[lag_row] for lag_row in range(8)], axis=1)
    high, low = split_values(grad * window[...])
    turned = dot(weights_kept[...], met(high, low, 0)) * cosine_second[...]
    high_second, low_second = split_values(turned)
    turned = dot(hidden_kept[...], met(high_second, low_second, 0)) * cosine_first[...]
    output_grad = lane_dot(met(high, low, 1), sine_second[...])
    hidden_grad = lane_dot(sine_first[...], met(high_second, low_second, 1))
    high, low = split_values(grad * slope[...])
    ones = jnp.ones((8, 2048), jnp.bfloat16)
    decay_row = lane_dot(ones, jnp.concatenate([high, low], axis=1))
    high, low = split_values(turned)
    embed_grad = lane_dot(table_kept[...], met(high, low, 1))

    shared = jnp.concatenate([hidden_grad, embed_grad], axis=1)
    for k in range(4):
        partial[:, k, :] = shared[16 * k : 16 * k + 16]
    packed = jnp.concatenate([output_grad[:32], output_grad[32:]], axis=1)
    for k in range(2):
        partial[:, 4 + k, :] = packed[16 * k : 16 * k + 16]
    decays = jnp.concatenate([decay_row[:1], jnp.zeros((1, 64), jnp.float32)], axis=1)
    partial[:, 6, :] = jnp.broadcast_to(decays, (16, 128))
    over_dp(2, lambda index: partial.at[index], lambda at: partials.at[me])
    partials[me] = partial[me]
    over_chan(0, lambda index: rows.at[index], lambda at: landed.at[group])
    landed[group] = rows[group]
    all_bytes(lags, dp_send.at[1], 15)
    all_bytes(rows, chan_send.at[0], 7)
    all_bytes(partials, dp_recv.at[2], 15)
    own_sum[...] = jnp.sum(partials[...], axis=0)
    over_chan(1, lambda index: own_sum, lambda at: group_sums.at[group])
    group_sums[group] = own_sum[...]
    all_bytes(group_sums, chan_recv.at[1], 7)
    summed = jnp.sum(group_sums[...], axis=0)
    piece[0:4, :] = summed[0:4]
    for g in range(8):
        piece[4 + 2 * g : 6 + 2 * g, :] = group_sums[g, 4:6, :]
    over_dp(3, lambda index: piece, lambda at: pieces.at[me])
    pieces[me] = piece[...]
    all_bytes(landed, chan_recv.at[0], 7)
    all_bytes(pieces, dp_recv.at[3], 15)
    all_bytes(partial, dp_send.at[2], 15)
    all_bytes(group_sums, chan_send.at[1], 7)
    all_bytes(pieces, dp_send.at[3], 15)


def finish(
    landed,
    pieces,
    group_sums,
    used,
    filter_out,
    embed_out,
    bias_out,
    hidden_out,
    frequency_out,
    output_out,
    decay_out,
    embed,
    bias,
    hidden,
    frequency,
    output_rows,
    output,
    decay,
    sems,
):
    copies = [pltpu.make_async_copy(landed, filter_out, sems.at[0])]
    copies[0].start()

    def send(source, target):
        copies.append(pltpu.make_async_copy(source, target, sems.at[len(copies)]))
        copies[-1].start()

    for g in range(8):
        for k in range(2):
            block = pieces[:, 4 + 2 * g + k, :]
            at = 64 * g + 16 * k
            output_rows[at : at + 16, :] = block[:, :64]
            output_rows[at + 32 : at + 48, :] = block[:, 64:]
    output[...] = output_rows[...].T
    send(output, output_out)
    shared = jnp.concatenate([pieces[:, k, :] for k in range(4)], axis=0)
    scales = jnp.concatenate([used[129:130, :], used[128:129, :]], axis=1)
    scaled = shared * scales
    embed[...] = scaled[:33, 64:]
    send(embed, embed_out)
    bias[...] = scaled[33:34, 64:]
    send(bias, bias_out)
    hidden[...] = scaled.T[:64]
    send(hidden, hidden_out)
    frequency[0:1, :] = jnp.sum(shared[:, 64:] * used[0:64, :], axis=0, keepdims=True)
    frequency[1:2, :] = jnp.sum(shared[:, :64] * used[64:128, :], axis=0, keepdims=True)
    send(frequency, frequency_out)
    for g in range(8):
        decay[0:1, 64 * g : 64 * g + 64] = group_sums[g, 6:7, :64]
    send(decay, decay_out)
    for copy in copies:
        copy.wait()


def local(
    signal,
    signal_grad,
    embed_weight,
    embed_bias,
    hidden_weight,
    frequency,
    output_weight,
    decay_rate,
):
    total = 2 * signal.shape[2]
    scale = 1.0 / math.sqrt(16 * signal.shape[2])
    factors = [max(1, int(0.45 * total * 10000.0 ** (-band / 16))) for band in range(16)]
    bands = np.repeat(np.array(factors, np.int32)[:, None], 128, axis=1)
    tables = transform_tables(total, scale)
    vmem = pl.BlockSpec(memory_space=pltpu.VMEM)
    f32 = jnp.float32
    lags = pltpu.VMEM((64, 1024), f32)
    halves = pltpu.VMEM((64, 3072), jnp.bfloat16)
    stored = [jnp.asarray(t) for t in tables] + [
        jnp.asarray(bands),
        embed_weight.T,
        embed_bias.reshape(1, 64),
        hidden_weight,
        frequency,
        output_weight.T,
        decay_rate.reshape(1, 512),
    ]
    hbm = pl.BlockSpec(memory_space=pltpu.HBM)
    landed, pieces, group_sums, used = pl.pallas_call(
        kernel,
        out_shape=[
            jax.ShapeDtypeStruct(shape, f32) for shape in [(8, 64, 128), (16, 20, 128), (8, 8, 128), (136, 64)]
        ],
        in_specs=[hbm] * 14,
        out_specs=[vmem] * 4,
        scratch_shapes=[
            *[pltpu.VMEM(t.shape, t.dtype) for t in stored],
            pltpu.VMEM((2, 4, 16, 8192), jnp.bfloat16),
            pltpu.VMEM((2, 1152, 128), f32),
            pltpu.VMEM((16, 4, 2, 64, 128), jnp.bfloat16),
            pltpu.VMEM((16, 4, 2, 64, 128), jnp.bfloat16),
            pltpu.VMEM((256, 256), f32),
            pltpu.VMEM((16, 8, 512), f32),
            pltpu.VMEM((16, 8, 512), f32),
            pltpu.VMEM((8, 64, 128), f32),
            lags,
            halves,
            pltpu.VMEM((64, 192), jnp.bfloat16),
            pltpu.VMEM((64, 192), jnp.bfloat16),
            pltpu.VMEM((64, 64), f32),
            pltpu.VMEM((512, 128), f32),
            pltpu.VMEM((512, 64), f32),
            halves,
            lags,
            halves,
            *[lags] * 3,
            pltpu.VMEM((16, 8, 128), f32),
            pltpu.VMEM((16, 8, 128), f32),
            pltpu.VMEM((8, 128), f32),
            pltpu.VMEM((20, 128), f32),
            pltpu.SemaphoreType.DMA,
            pltpu.SemaphoreType.DMA((8,)),
            pltpu.SemaphoreType.DMA((12,)),
            pltpu.SemaphoreType.REGULAR((3,)),
            pltpu.SemaphoreType.DMA((15,)),
            pltpu.SemaphoreType.DMA((4,)),
            pltpu.SemaphoreType.DMA((4,)),
            pltpu.SemaphoreType.DMA((2,)),
            pltpu.SemaphoreType.DMA((2,)),
        ],
        compiler_params=pltpu.CompilerParams(
            collective_id=0, has_side_effects=True, vmem_limit_bytes=40 * 1024 * 1024
        ),
    )(*[pltpu.with_memory_space_constraint(t, pltpu.HBM) for t in (signal[0], signal_grad[0], *stored)])
    shapes = [(512, 128), (33, 64), (1, 64), (64, 64), (2, 64), (64, 512), (1, 512)]
    outs = pl.pallas_call(
        finish,
        out_shape=[jax.ShapeDtypeStruct(shape, f32) for shape in shapes],
        in_specs=[vmem] * 4,
        out_specs=[hbm] * 7,
        scratch_shapes=[
            *[pltpu.VMEM(shape, f32) for shape in shapes[1:5]],
            pltpu.VMEM((512, 64), f32),
            *[pltpu.VMEM(shape, f32) for shape in shapes[5:]],
            pltpu.SemaphoreType.DMA((7,)),
        ],
        compiler_params=pltpu.CompilerParams(vmem_limit_bytes=8 * 1024 * 1024),
    )(landed.reshape(512, 128), pieces, group_sums, used)
    lag_grad, embed_grad, bias_grad, hidden_grad, frequency_grad, output_grad, decay_grad = outs
    return (
        lag_grad,
        embed_grad.T,
        bias_grad.reshape(64),
        hidden_grad,
        frequency_grad,
        output_grad.T,
        decay_grad.reshape(512),
    )


def solution(mesh):
    torus = Mesh(mesh.devices.reshape(4, 4, 4, 2), ("y", "x", "z", "core"))
    return jax.shard_map(
        local,
        mesh=torus,
        in_specs=(P(DP, CHAN, None), P(DP, CHAN, None), P(), P(), P(), P(), P(), P()),
        out_specs=(P(None, DP + CHAN), P(), P(), P(), P(), P(), P()),
        check_vma=False,
    )
```
